32 devices in a mesh: section: 2 (over x), dp: 16 (over z, y, core).
Axes of the slice: x: 2, y: 2, z: 4, core: 2. Of those that a mesh axis runs over, the one named last changes fastest.
Arguments:
- inputs: bfloat16 [12288, 768], P('dp'), may hold values from -6 to 6
- out_cotangent: bfloat16 [12288, 768], P('dp'), may hold values from -6 to 6
- sequence_ids: int32 [48, 256], P('dp'), may hold values from 0 to 7, never falling along the last dimension, each value on 1 to 128 neighbouring positions
- w_qk: bfloat16 [2, 768, 1536], P('section'), may hold values from -0.21875 to 0.21875
- w_value: bfloat16 [2, 768, 768], P('section'), may hold values from -0.375 to 0.375
- w_out: bfloat16 [2, 768, 768], P('section'), may hold values from -0.375 to 0.375
- w_up: bfloat16 [2, 768, 3072], P('section'), may hold values from -0.375 to 0.375
- w_down: bfloat16 [2, 3072, 768], P('section'), may hold values from -0.1875 to 0.1875
- norm_gains: float32 [2, 3, 768], P('section'), may hold values from 0.1 to 1.9
- norm_shifts: float32 [2, 3, 768], P('section'), may hold values from -2 to 2
- ffn_gain: float32 [2, 3072], P('section'), may hold values from 0.1 to 1.9
- ffn_shift: float32 [2, 3072], P('section'), may hold values from -2 to 2
- proj_bias: float32 [2, 4, 768], P('section'), may hold values from -2 to 2
- up_bias: float32 [2, 3072], P('section'), may hold values from -2 to 2
Outputs:
- layer_outputs: bfloat16 [2, 12288, 768], P('section', 'dp')
- input_grads: bfloat16 [2, 12288, 768], P('section', 'dp')
- grad_qk: float32 [2, 768, 1536], P('section', 'dp')
- grad_value: float32 [2, 768, 768], P('section', 'dp')
- grad_out: float32 [2, 768, 768], P('section', 'dp')
- grad_up: float32 [2, 768, 3072], P('section', 'dp')
- grad_down: float32 [2, 3072, 768], P('section', 'dp')
- grad_gains: float32 [2, 3, 768], P('section', None, 'dp')
- grad_shifts: float32 [2, 3, 768], P('section', None, 'dp')
- grad_ffn_gain: float32 [2, 3072], P('section', 'dp')
- grad_ffn_shift: float32 [2, 3072], P('section', 'dp')
- grad_proj_bias: float32 [2, 4, 768], P('section', None, 'dp')
- grad_up_bias: float32 [2, 3072], P('section', 'dp')
The draws below stay inside these ranges and needn't reach their ends.
Inputs may be any that keep to these rules, and one draw needn't show every extreme that they name: In each row of sequence_ids the ids never fall; each sequence has 1 to 128 tokens and some sequence has exactly 128.
All inputs are finite; a program needn't handle non-finite values.
Results may differ from the reference program's by a relative error of at most 0.023.
Values may be sent and summed in bfloat16 or wider, within the bound.
No kernel may reach another device: no remote copies, remote signals or barrier semaphores. Data moves between devices by JAX's collectives and lax.ppermute only.
A program may use at most 256 MiB of HBM per device.

```python
import math
import jax
import jax.numpy as jnp
import numpy as np
from jax import lax

D = 768
HEADS = 12
HEAD_DIM = 64
FF = 3072
MB_ROWS = 256
MICRO = 3
SEGS = 8
SEG_MOST = 128
TOKENS = 12288
N_DP = 16


def level_of(own_key, extent, pieces, low, high):
    factor_of = 1.0
    for axis_at, parts in pieces:
        heights = jax.random.uniform(jax.random.fold_in(jax.random.fold_in(own_key, 6), axis_at), (parts,), jnp.float32, low / len(pieces), high / len(pieces))
        factor_of = factor_of * jnp.repeat(jnp.exp(heights), extent[axis_at] // parts).reshape((-1,) + (1,) * (len(extent) - 1 - axis_at))
    return factor_of


def split_up(count, total, limit, skew):
    weights = [(1 << 20) // math.isqrt(standing ** skew) + 1 for standing in range(2, count + 1)]
    rest, holding = total - limit - (count - 1), [1] * (count - 1)
    while rest > 0:
        free = [i for i in range(count - 1) if holding[i] < limit]
        pool, remaining = sum([weights[i] for i in free]), rest
        for i in free:
            more = min(limit - holding[i], max(1, remaining * weights[i] // pool), rest)
            holding[i] = holding[i] + more
            rest = rest - more
    return np.array([limit] + holding)


def uneven(own_key, count, total, most, skew):
    if count == 2:
        one = jax.random.randint(own_key, (), max(1, total - most), min(most, total - 1) + 1)
        return jnp.stack([one, total - one])
    sizes = jnp.asarray(split_up(count, total, most, skew), jnp.int32)
    twos = (count - 1) // 2
    source_of, sink = sizes[1:1 + 2 * twos:2], sizes[2:2 + 2 * twos:2]
    room = jnp.minimum(source_of - 1, most - sink)
    shifted = jax.random.randint(jax.random.fold_in(own_key, 1), (twos,), 0, 1 << 20) % (room + 1)
    sizes = sizes.at[1:1 + 2 * twos:2].set(source_of - shifted).at[2:2 + 2 * twos:2].set(sink + shifted)
    return sizes[jax.random.permutation(jax.random.fold_in(own_key, 2), count)]


def scatter_about(own_key, dims, width, reach, pieces=(), held_as=jnp.bfloat16):
    values = width * jax.random.normal(own_key, dims, jnp.float32)
    if pieces:
        values = values * level_of(own_key, dims, pieces, -0.22, 0.18)
    return jnp.clip(values, -reach, reach).astype(held_as)


def setup_inputs(seed: int = 0) -> dict:
    splits = jax.random.split(jax.random.key(seed), 15)
    inputs = scatter_about(splits[0], (TOKENS, D), 1.0, 6.0, ((0, 16),))
    out_cotangent = scatter_about(splits[1], (TOKENS, D), 1.0, 6.0, ((0, 16),))
    sequence_ids = jax.vmap(lambda own: jnp.searchsorted(jnp.cumsum(uneven(own, SEGS, MB_ROWS, SEG_MOST, 2)), jnp.arange(MB_ROWS), side="right"))(jax.random.split(splits[2], (N_DP * MICRO))).reshape((N_DP * MICRO, MB_ROWS)).astype(jnp.int32)
    w_qk = scatter_about(splits[3], (2, D, 2 * D), D ** -0.5, 0.21875, ((0, 2),))
    w_value = scatter_about(splits[4], (2, D, D), (D * 1000 // 3178) ** -0.5, 0.375, ((0, 2),))
    w_out = scatter_about(splits[5], (2, D, D), (D * 1000 // 3178) ** -0.5, 0.375, ((0, 2),))
    w_up = scatter_about(splits[6], (2, D, FF), (D * 1000 // 3178) ** -0.5, 0.375, ((0, 2),))
    w_down = scatter_about(splits[7], (2, FF, D), (FF * 1000 // 3178) ** -0.5, 0.1875, ((0, 2),))
    norm_gains = jnp.clip(1.0 + 0.18 * jax.random.normal(splits[8], (2, 3, D), jnp.float32), 0.1, 1.9)
    norm_shifts = scatter_about(splits[9], (2, 3, D), 0.3, 2.0, ((0, 2),), jnp.float32)
    ffn_gain = jnp.clip(1.0 + 0.18 * jax.random.normal(splits[10], (2, FF), jnp.float32), 0.1, 1.9)
    ffn_shift = scatter_about(splits[11], (2, FF), 0.3, 2.0, ((0, 2),), jnp.float32)
    proj_bias = scatter_about(splits[12], (2, 4, D), 0.3, 2.0, ((0, 2),), jnp.float32)
    up_bias = scatter_about(splits[13], (2, FF), 0.3, 2.0, ((0, 2),), jnp.float32)
    return {"inputs": inputs, "out_cotangent": out_cotangent, "sequence_ids": sequence_ids, "w_qk": w_qk, "w_value": w_value, "w_out": w_out, "w_up": w_up, "w_down": w_down, "norm_gains": norm_gains, "norm_shifts": norm_shifts, "ffn_gain": ffn_gain, "ffn_shift": ffn_shift, "proj_bias": proj_bias, "up_bias": up_bias}


norm_eps = 1e-05
masked_score = -1e+30

@jax.custom_vjp
def low(v):
    return lax.optimization_barrier(v.astype(jnp.bfloat16)).astype(jnp.float32)

@jax.custom_vjp
def low_back(v):
    return v

def low_keep(v):
    return (low(v), None)

def low_pass(kept, grad):
    return (grad,)

def back_keep(v):
    return (v, None)

def back_low(kept, grad):
    return (low(grad),)
low.defvjp(low_keep, low_pass)
low_back.defvjp(back_keep, back_low)

def matmul(left, right):
    return jnp.dot(left, right, precision=lax.Precision.HIGHEST, preferred_element_type=jnp.float32)

def layer_norm(values, gain, shift):
    center = values - lax.optimization_barrier(jnp.mean(values, axis=-1, keepdims=True))
    spread = lax.optimization_barrier(jnp.mean(center * center, axis=-1, keepdims=True))
    return center * lax.rsqrt(spread + norm_eps) * gain + shift

def attend_block(queries, key_rows, value_rows, seq_ids):
    rows = queries.shape[0]
    query_heads = queries.reshape(rows, HEADS, HEAD_DIM)
    key_heads = key_rows.reshape(rows, HEADS, HEAD_DIM)
    value_heads = value_rows.reshape(rows, HEADS, HEAD_DIM)
    scores = jnp.einsum('qhd,khd->hqk', query_heads, key_heads, precision=lax.Precision.HIGHEST) * HEAD_DIM ** (-0.5)
    scores = low_back(scores)
    same_seq = seq_ids[:, None] == seq_ids[None, :]
    scores = jnp.where(same_seq[None], scores, masked_score)
    top_score = lax.optimization_barrier(jnp.max(scores, axis=-1, keepdims=True))
    lifted = jnp.exp(scores - top_score)
    attn_probs = low(lifted / lax.optimization_barrier(jnp.sum(lifted, axis=-1, keepdims=True)))
    mixed = jnp.einsum('hqk,khd->qhd', attn_probs, value_heads, precision=lax.Precision.HIGHEST)
    return mixed.reshape(rows, HEADS * HEAD_DIM)

def block_attend(packed):
    return jax.checkpoint(attend_block)(packed[0], packed[1], packed[2], packed[3])

def layer(start, params, seq_ids):
    w_qk, w_value, w_out, w_up, w_down, gains, shifts, ffn_gain, ffn_shift, proj_bias, up_bias = params
    normed = low(layer_norm(start, gains[0], shifts[0]))
    joint = matmul(normed, w_qk)
    queries = low_back(low(joint[:, :D] + proj_bias[0]))
    key_rows = low_back(low(joint[:, D:]))
    value_rows = low_back(low(matmul(normed, w_value) + proj_bias[1]))
    packed = (queries.reshape(-1, MB_ROWS, D), key_rows.reshape(-1, MB_ROWS, D), value_rows.reshape(-1, MB_ROWS, D), seq_ids)
    mixed = lax.map(block_attend, packed)
    mixed = low_back(mixed.reshape(-1, D))
    mixed_normed = low(layer_norm(mixed, gains[1], shifts[1]))
    middle = start + low_back(matmul(mixed_normed, w_out) + proj_bias[2])
    ffn_in = low(layer_norm(middle, gains[2], shifts[2]))
    hidden = low_back(matmul(ffn_in, w_up) + up_bias)
    hidden_normed = low(layer_norm(jax.nn.gelu(hidden, approximate=False), ffn_gain, ffn_shift))
    return middle + low_back(matmul(hidden_normed, w_down) + proj_bias[3])

def reference(inputs, out_cotangent, sequence_ids, w_qk, w_value, w_out, w_up, w_down, norm_gains, norm_shifts, ffn_gain, ffn_shift, proj_bias, up_bias):
    stacked = (w_qk, w_value, w_out, w_up, w_down, norm_gains, norm_shifts, ffn_gain, ffn_shift, proj_bias, up_bias)
    first_params = tuple((member[0].astype(jnp.float32) for member in stacked))
    second_params = tuple((member[1].astype(jnp.float32) for member in stacked))

    def run_layer(start, params):
        return layer(start, params, sequence_ids)
    first_out, first_back = jax.vjp(run_layer, inputs.astype(jnp.float32), first_params)
    passed = first_out.astype(jnp.bfloat16).astype(jnp.float32)
    second_out, second_back = jax.vjp(run_layer, passed, second_params)
    carried, second_grads = second_back(out_cotangent.astype(jnp.float32))
    carried = carried.astype(jnp.bfloat16)
    start_grad, first_grads = first_back(carried.astype(jnp.float32))
    layer_outputs = jnp.stack([first_out.astype(jnp.bfloat16), second_out.astype(jnp.bfloat16)])
    input_grads = jnp.stack([start_grad.astype(jnp.bfloat16), carried])
    grads = [jnp.stack([first_grads[index], second_grads[index]]) for index in range(11)]
    return (layer_outputs, input_grads, grads[0], grads[1], grads[2], grads[3], grads[4], grads[5], grads[6], grads[7], grads[8], grads[9], grads[10])
```

```python
import functools

import jax
import jax.numpy as jnp
from jax import lax
from jax.experimental import pallas as pl
from jax.experimental.pallas import tpu as pltpu
from jax.sharding import PartitionSpec as P

D = 768
HEADS = 12
HEAD_DIM = 64
FF = 3072
ROWS = 256
MICRO = 3
EPS = 1e-05
MASKED = -1e30
CH = 512
N_CH = FF // CH
PAIRS = HEADS // 2
F32 = jnp.float32
BF16 = jnp.bfloat16
ANY = pl.BlockSpec(memory_space=pl.ANY)
VM = pl.BlockSpec(memory_space=pltpu.VMEM)
SM = pl.BlockSpec(memory_space=pltpu.SMEM)


def dot_nn(a, b):
    return lax.dot_general(a, b, (((1,), (0,)), ((), ())), preferred_element_type=F32)


def dot_nt(a, b):
    return lax.dot_general(a, b, (((1,), (1,)), ((), ())), preferred_element_type=F32)


def dot_tn(a, b):
    return lax.dot_general(a, b, (((0,), (0,)), ((), ())), preferred_element_type=F32)


def center_spread(v):
    c = v - jnp.mean(v, axis=-1, keepdims=True)
    r = lax.rsqrt(jnp.mean(c * c, axis=-1, keepdims=True) + EPS)
    return c, r


def norm(v, gain, shift):
    c, r = center_spread(v)
    return c * r * gain + shift


def norm_back(grad, v, gain):
    c, r = center_spread(v)
    x = c * r
    h = grad * gain
    back = r * (h - jnp.mean(h, axis=-1, keepdims=True) - x * jnp.mean(h * x, axis=-1, keepdims=True))
    return back, colsum(grad * x), colsum(grad)


def colsum(v):
    return jnp.sum(v, axis=0, keepdims=True)


def lane_fold(v):
    total = v[:, :128]
    for k in range(1, v.shape[1] // 128):
        total = total + v[:, k * 128 : (k + 1) * 128]
    return total


def same_bias(seq_row):
    rows = jnp.broadcast_to(seq_row.astype(F32), (ROWS, ROWS))
    return jnp.where(rows == rows.T, 0.0, MASKED)


def aligned(i, size):
    return pl.ds(pl.multiple_of(i * size, size), size)


class Copies:
    def __init__(self, sems):
        self.sems = sems
        self.count = 0
        self.open = []

    def start(self, src, dst, kept=False):
        copy = pltpu.make_async_copy(src, dst, self.sems.at[self.count])
        self.count += 1
        copy.start()
        if kept:
            self.open.append(copy)
        return copy

    def finish(self):
        for copy in self.open:
            copy.wait()


F_STATE = (
    ("src", D, BF16),
    ("normed", D, BF16),
    ("qkv", 3 * D, BF16),
    ("mixed", D, BF16),
    ("mnormed", D, BF16),
    ("middle", D, BF16),
    ("ffn_in", D, BF16),
    ("xh", FF, BF16),
    ("hn", FF, BF16),
    ("gp", FF, BF16),
    ("rst", 128, F32),
    ("louts", D, BF16),
)
B_STATE = (
    ("dh", FF, BF16),
    ("gml", D, BF16),
    ("gqkv", 3 * D, BF16),
    ("igr", D, BF16),
)


def forward_kernel(n_alias, *refs):
    (scal, inp_all, recv, seq, wqk_h, wv_h, wout_h, wup_h, wdown_h) = refs[:9]
    gains, shifts, fg, fs, pb, ub = refs[9:15]
    refs = refs[15 + n_alias :]
    outs = dict(zip([s[0] for s in F_STATE], refs[:12]))
    res = refs[12]
    stage = dict(zip([s[0] for s in F_STATE], refs[13:25]))
    wqk, wv, wout, wup, wdown, act, bias, acc, mid, sems = refs[25:35]
    active, mb, sec = scal[0], scal[1], scal[2]

    @pl.when(active == 1)
    def _():
        cp = Copies(sems)

        def save(name):
            cp.start(stage[name], outs[name].at[mb], kept=True)

        src_copy = pltpu.make_async_copy(recv, stage["src"], sems.at[20])

        @pl.when(sec == 0)
        def _():
            pltpu.make_async_copy(inp_all.at[mb], stage["src"], sems.at[20]).start()

        @pl.when(sec != 0)
        def _():
            src_copy.start()

        w1 = cp.start(wqk_h, wqk)
        w2 = cp.start(wv_h, wv)
        w3 = cp.start(wout_h, wout)
        w4 = cp.start(wup_h, wup)
        w5 = cp.start(wdown_h, wdown)
        bias[...] = same_bias(seq[mb])
        src_copy.wait()
        save("src")
        u = stage["src"][...].astype(F32)
        normed = norm(u, gains[0:1], shifts[0:1]).astype(BF16)
        stage["normed"][...] = normed
        save("normed")
        qkv = stage["qkv"]
        w1.wait()
        qkv[:, 0:D] = ((dot_nn(normed, wqk[:, 0:D]) + pb[0:1]).astype(BF16)) * 0.125
        qkv[:, D : 2 * D] = dot_nn(normed, wqk[:, D : 2 * D]).astype(BF16)
        w2.wait()
        qkv[:, 2 * D :] = (dot_nn(normed, wv[...]) + pb[1:2]).astype(BF16)
        save("qkv")
        low = lax.broadcasted_iota(jnp.int32, (ROWS, 128), 1) < HEAD_DIM

        def pair(j, _):
            q2 = qkv[:, aligned(j, 128)]
            k2 = qkv[:, aligned(j + PAIRS, 128)]
            v2 = qkv[:, aligned(j + 2 * PAIRS, 128)]
            zero = jnp.zeros_like(k2)
            one = jnp.ones_like(v2)
            sums = []
            for first in (True, False):
                kh = jnp.where(low, k2, zero) if first else jnp.where(low, zero, k2)
                vh = jnp.where(low, v2, one) if first else jnp.where(low, one, v2)
                scores = dot_nt(q2, kh) + bias[...]
                lifted = jnp.exp(scores - jnp.max(scores, axis=-1, keepdims=True)).astype(BF16)
                sums.append(dot_nn(lifted, vh))
            top = jnp.where(low, sums[0], sums[1])
            den = pltpu.roll(jnp.where(low, sums[1], sums[0]), 64, 1)
            mid[:, aligned(j, 128)] = top / den
            return 0

        lax.fori_loop(0, PAIRS, pair, 0)
        mixed = mid[...]
        stage["mixed"][...] = mixed.astype(BF16)
        save("mixed")
        mnormed = norm(mixed, gains[1:2], shifts[1:2]).astype(BF16)
        stage["mnormed"][...] = mnormed
        save("mnormed")
        w3.wait()
        middle = stage["src"][...].astype(F32) + dot_nn(mnormed, wout[...]) + pb[2:3]
        mid[...] = middle
        stage["middle"][...] = middle.astype(BF16)
        save("middle")
        ffn_in = norm(middle, gains[2:3], shifts[2:3]).astype(BF16)
        stage["ffn_in"][...] = ffn_in
        save("ffn_in")
        w4.wait()

        def up(i, total):
            at = aligned(i, CH)
            h = dot_nn(stage["ffn_in"][...], wup[:, at]) + ub[:, at]
            cdf = 0.5 + 0.5 * lax.erf(h * 0.7071067811865476)
            a = h * cdf
            act[:, at] = a
            pdf = jnp.exp(h * h * -0.5) * 0.3989422804014327
            stage["gp"][:, at] = (cdf + h * pdf).astype(BF16)
            return total + lane_fold(a)

        total = lax.fori_loop(0, N_CH, up, jnp.zeros((ROWS, 128), F32))
        save("gp")
        mean = jnp.sum(total, axis=-1, keepdims=True) * (1.0 / FF)

        def spread(i, total):
            c = act[:, aligned(i, CH)] - mean
            return total + lane_fold(c * c)

        total = lax.fori_loop(0, N_CH, spread, jnp.zeros((ROWS, 128), F32))
        r = lax.rsqrt(jnp.sum(total, axis=-1, keepdims=True) * (1.0 / FF) + EPS)
        stage["rst"][...] = jnp.broadcast_to(r, (ROWS, 128))
        save("rst")
        w5.wait()
        acc[...] = mid[...] + pb[3:4]

        def down(i, _):
            at = aligned(i, CH)
            x = (act[:, at] - mean) * r
            stage["xh"][:, at] = x.astype(BF16)
            hn = (x * fg[:, at] + fs[:, at]).astype(BF16)
            stage["hn"][:, at] = hn
            acc[...] += dot_nn(hn, wdown[at, :])
            return 0

        lax.fori_loop(0, N_CH, down, 0)
        save("xh")
        save("hn")
        result = acc[...].astype(BF16)
        res[...] = result
        stage["louts"][...] = result
        save("louts")
        cp.finish()


def forward_call(scal, inp_all, recv, seq, params, state):
    alias = [] if state is None else list(state)
    n_in = 15
    out_shape = [jax.ShapeDtypeStruct((MICRO, ROWS, n), t) for _, n, t in F_STATE]
    out_shape.append(jax.ShapeDtypeStruct((ROWS, D), BF16))
    scratch = [pltpu.VMEM((ROWS, n), t) for _, n, t in F_STATE]
    scratch += [
        pltpu.VMEM((D, 2 * D), BF16),
        pltpu.VMEM((D, D), BF16),
        pltpu.VMEM((D, D), BF16),
        pltpu.VMEM((D, FF), BF16),
        pltpu.VMEM((FF, D), BF16),
        pltpu.VMEM((ROWS, FF), F32),
        pltpu.VMEM((ROWS, ROWS), F32),
        pltpu.VMEM((ROWS, D), F32),
        pltpu.VMEM((ROWS, D), F32),
        pltpu.SemaphoreType.DMA((21,)),
    ]
    outs = pl.pallas_call(
        functools.partial(forward_kernel, len(alias)),
        name="layer_forward",
        out_shape=out_shape,
        in_specs=[SM, ANY, ANY, VM] + [ANY] * 5 + [VM] * 6 + [ANY] * len(alias),
        out_specs=[ANY] * 12 + [VM],
        scratch_shapes=scratch,
        input_output_aliases={n_in + i: i for i in range(len(alias))},
        compiler_params=pltpu.CompilerParams(vmem_limit_bytes=56 << 20),
        cost_estimate=pl.CostEstimate(flops=4 * 10**9, bytes_accessed=24 << 20, transcendentals=2 * 10**6),
    )(scal, inp_all, recv, seq, *params, *alias)
    return outs[:12], outs[12]


def backward_kernel(n_alias, *refs):
    (scal, cot_all, recv, seq, wqk_h, wv_h, wout_h, wup_h, wdown_h) = refs[:9]
    gains, fg = refs[9:11]
    src_h, qkv_h, mixed_h, middle_h, xh_h, gp_h, rst_h = refs[11:18]
    refs = refs[18 + n_alias :]
    dh_o, gml_o, gqkv_o, igr_o, vec_o, vecf_o, send = refs[:7]
    dh, gml, gqkv, igr, vec, vecf = refs[7:13]
    gy_b, src, qkv, mixed, middle, xh, gp, rst = refs[13:21]
    wqk, wv, wout, wup, wdown, act, bias, acc, mid, gmix, sems = refs[21:32]
    active, mb, sec = scal[0], scal[1], scal[2]

    @pl.when(active == 1)
    def _():
        cp = Copies(sems)
        gy_copy = pltpu.make_async_copy(recv, gy_b, sems.at[20])

        @pl.when(sec == 0)
        def _():
            gy_copy.start()

        @pl.when(sec != 0)
        def _():
            pltpu.make_async_copy(cot_all.at[mb], gy_b, sems.at[20]).start()

        w5 = cp.start(wdown_h, wdown)
        c_xh = cp.start(xh_h.at[mb], xh)
        c_gp = cp.start(gp_h.at[mb], gp)
        c_rst = cp.start(rst_h.at[mb], rst)
        w4 = cp.start(wup_h, wup)
        c_mid = cp.start(middle_h.at[mb], middle)
        w3 = cp.start(wout_h, wout)
        c_mix = cp.start(mixed_h.at[mb], mixed)
        c_qkv = cp.start(qkv_h.at[mb], qkv)
        w1 = cp.start(wqk_h, wqk)
        w2 = cp.start(wv_h, wv)
        c_src = cp.start(src_h.at[mb], src)
        bias[...] = same_bias(seq[mb])
        gy_copy.wait()
        w5.wait()
        c_xh.wait()
        vec[9:10] = colsum(gy_b[...].astype(F32))

        def first(i, totals):
            at = aligned(i, CH)
            g = dot_nt(gy_b[...], wdown[at, :])
            x = xh[:, at].astype(F32)
            gx = g * x
            vecf[0:1, at] = colsum(gx)
            vecf[1:2, at] = colsum(g)
            h = g * fg[:, at]
            act[:, at] = h
            return totals[0] + lane_fold(h), totals[1] + lane_fold(h * x)

        zeros = jnp.zeros((ROWS, 128), F32)
        t1, t2 = lax.fori_loop(0, N_CH, first, (zeros, zeros))
        m1 = jnp.sum(t1, axis=-1, keepdims=True) * (1.0 / FF)
        m2 = jnp.sum(t2, axis=-1, keepdims=True) * (1.0 / FF)
        c_gp.wait()
        c_rst.wait()
        w4.wait()
        r = rst[:, 0:1]
        acc[...] = jnp.zeros_like(acc)

        def second(i, _):
            at = aligned(i, CH)
            x = xh[:, at].astype(F32)
            d = (act[:, at] - m1 - x * m2) * r * gp[:, at].astype(F32)
            vecf[2:3, at] = colsum(d)
            low_d = d.astype(BF16)
            dh[:, at] = low_d
            acc[...] += dot_nt(low_d, wup[:, at])
            return 0

        lax.fori_loop(0, N_CH, second, 0)
        cp.start(dh, dh_o.at[mb], kept=True)
        cp.start(vecf, vecf_o.at[mb], kept=True)
        c_mid.wait()
        back, v_gain, v_shift = norm_back(acc[...], middle[...].astype(F32), gains[2:3])
        vec[2:3] = v_gain
        vec[5:6] = v_shift
        gm = gy_b[...].astype(F32) + back
        mid[...] = gm
        gml_v = gm.astype(BF16)
        gml[...] = gml_v
        cp.start(gml, gml_o.at[mb], kept=True)
        vec[8:9] = colsum(gm)
        w3.wait()
        c_mix.wait()
        back, v_gain, v_shift = norm_back(dot_nt(gml_v, wout[...]), mixed[...].astype(F32), gains[1:2])
        vec[1:2] = v_gain
        vec[4:5] = v_shift
        gmix[...] = back.astype(BF16)
        c_qkv.wait()
        low = lax.broadcasted_iota(jnp.int32, (ROWS, 128), 1) < HEAD_DIM

        def pair(j, _):
            q2 = qkv[:, aligned(j, 128)]
            k2 = qkv[:, aligned(j + PAIRS, 128)]
            v2 = qkv[:, aligned(j + 2 * PAIRS, 128)]
            g2 = gmix[:, aligned(j, 128)]
            zero = jnp.zeros_like(k2)
            gq = gk = gv = None
            for head in range(2):

                def half(t):
                    return jnp.where(low, t, zero) if head == 0 else jnp.where(low, zero, t)

                kh, vh, qh, gh = half(k2), half(v2), half(q2), half(g2)
                st = dot_nt(kh, q2) + bias[...]
                e = jnp.exp(st - jnp.max(st, axis=0, keepdims=True))
                p = e * (1.0 / jnp.sum(e, axis=0, keepdims=True))
                gp_t = dot_nt(vh, g2)
                inner = jnp.sum(p * gp_t, axis=0, keepdims=True)
                gs = (p * (gp_t - inner)).astype(BF16)
                a = dot_nn(p.astype(BF16), gh)
                b = dot_nn(gs, qh)
                c = dot_tn(gs, kh * 0.125)
                gv = a if gv is None else gv + a
                gk = b if gk is None else gk + b
                gq = c if gq is None else gq + c
            gqkv[:, aligned(j, 128)] = gq.astype(BF16)
            gqkv[:, aligned(j + PAIRS, 128)] = gk.astype(BF16)
            gqkv[:, aligned(j + 2 * PAIRS, 128)] = gv.astype(BF16)
            vec[6:7, aligned(j, 128)] = colsum(gq)
            vec[7:8, aligned(j, 128)] = colsum(gv)
            return 0

        lax.fori_loop(0, PAIRS, pair, 0)
        cp.start(gqkv, gqkv_o.at[mb], kept=True)
        w1.wait()
        w2.wait()
        c_src.wait()
        gn = dot_nt(gqkv[:, : 2 * D], wqk[...]) + dot_nt(gqkv[:, 2 * D :], wv[...])
        back, v_gain, v_shift = norm_back(gn, src[...].astype(F32), gains[0:1])
        vec[0:1] = v_gain
        vec[3:4] = v_shift
        cp.start(vec, vec_o.at[mb], kept=True)
        out = (mid[...] + back).astype(BF16)
        send[...] = out
        igr[...] = out
        cp.start(igr, igr_o.at[mb], kept=True)
        cp.finish()


def backward_call(scal, cot_all, recv, seq, params, fstate, state):
    alias = [] if state is None else list(state)
    names = [s[0] for s in F_STATE]
    saved = [fstate[names.index(n)] for n in ("src", "qkv", "mixed", "middle", "xh", "gp", "rst")]
    wqk, wv, wout, wup, wdown, gains, shifts, fg, fs, pb, ub = params
    out_shape = [jax.ShapeDtypeStruct((MICRO, ROWS, n), t) for _, n, t in B_STATE]
    out_shape += [
        jax.ShapeDtypeStruct((MICRO, 16, D), F32),
        jax.ShapeDtypeStruct((MICRO, 8, FF), F32),
        jax.ShapeDtypeStruct((ROWS, D), BF16),
    ]
    scratch = [pltpu.VMEM((ROWS, n), t) for _, n, t in B_STATE]
    scratch += [pltpu.VMEM((16, D), F32), pltpu.VMEM((8, FF), F32)]
    scratch += [
        pltpu.VMEM((ROWS, n), t)
        for n, t in ((D, BF16), (D, BF16), (3 * D, BF16), (D, BF16), (D, BF16), (FF, BF16), (FF, BF16), (128, F32))
    ]
    scratch += [
        pltpu.VMEM((D, 2 * D), BF16),
        pltpu.VMEM((D, D), BF16),
        pltpu.VMEM((D, D), BF16),
        pltpu.VMEM((D, FF), BF16),
        pltpu.VMEM((FF, D), BF16),
        pltpu.VMEM((ROWS, FF), F32),
        pltpu.VMEM((ROWS, ROWS), F32),
        pltpu.VMEM((ROWS, D), F32),
        pltpu.VMEM((ROWS, D), F32),
        pltpu.VMEM((ROWS, D), BF16),
        pltpu.SemaphoreType.DMA((21,)),
    ]
    outs = pl.pallas_call(
        functools.partial(backward_kernel, len(alias)),
        name="layer_backward",
        out_shape=out_shape,
        in_specs=[SM, ANY, ANY, VM] + [ANY] * 5 + [VM] * 2 + [ANY] * 7 + [ANY] * len(alias),
        out_specs=[ANY] * 6 + [VM],
        scratch_shapes=scratch,
        input_output_aliases={18 + i: i for i in range(len(alias))},
        compiler_params=pltpu.CompilerParams(vmem_limit_bytes=60 << 20),
        cost_estimate=pl.CostEstimate(flops=5 * 10**9, bytes_accessed=24 << 20, transcendentals=10**6),
    )(scal, cot_all, recv, seq, wqk, wv, wout, wup, wdown, gains, fg, *saved, *alias)
    return outs[:6], outs[6]


TOK = MICRO * ROWS


def down_kernel(scal, hn, cot, q0, q1, q2, send, keep, gy, acc, sems):
    @pl.when(pl.program_id(0) == 0)
    def _():
        @pl.when(scal[1] == 0)
        def _():
            copies = [
                pltpu.make_async_copy(q, gy.at[pl.ds(i * ROWS, ROWS)], sems.at[i])
                for i, q in enumerate((q0, q1, q2))
            ]
            for c in copies:
                c.start()
            for c in copies:
                c.wait()

        @pl.when(scal[1] != 0)
        def _():
            c = pltpu.make_async_copy(cot, gy, sems.at[0])
            c.start()
            c.wait()

    half = acc.shape[0] // 2
    acc[...] = dot_tn(hn[...], gy[...])
    core = scal[0]
    send[0] = acc[pl.ds(pl.multiple_of((1 - core) * half, half), half), :].astype(BF16)
    keep[0] = acc[pl.ds(pl.multiple_of(core * half, half), half), :].astype(BF16)


def down_call(scal, hn, cot, qs, n_dp):
    rows = FF // n_dp
    half = n_dp // 2
    shape = jax.ShapeDtypeStruct((half, rows, D), BF16)
    spec = pl.BlockSpec((1, rows, D), lambda i: (i, 0, 0))
    return pl.pallas_call(
        down_kernel,
        name="grad_down",
        grid=(half,),
        out_shape=[shape, shape],
        in_specs=[SM, pl.BlockSpec((TOK, 2 * rows), lambda i: (0, i)), ANY, ANY, ANY, ANY],
        out_specs=[spec, spec],
        scratch_shapes=[
            pltpu.VMEM((TOK, D), BF16),
            pltpu.VMEM((2 * rows, D), F32),
            pltpu.SemaphoreType.DMA((3,)),
        ],
        compiler_params=pltpu.CompilerParams(vmem_limit_bytes=40 << 20),
        cost_estimate=pl.CostEstimate(flops=2 * TOK * D * FF, bytes_accessed=10 << 20, transcendentals=0),
    )(scal, hn.reshape(TOK, FF), cot.reshape(TOK, D), *qs)


def split_rows(scal, acc, send, keep):
    half, rows = send.shape[0], send.shape[1]
    core = scal[0]
    for j in range(half):
        send[j] = acc[pl.ds(pl.multiple_of((2 * j + 1 - core) * rows, rows), rows), :].astype(BF16)
        keep[j] = acc[pl.ds(pl.multiple_of((2 * j + core) * rows, rows), rows), :].astype(BF16)


def up_kernel(scal, left, right, send, keep, turned, acc):
    @pl.when(pl.program_id(0) == 0)
    def _():
        turned[...] = left[...].T

    acc[...] = dot_nn(turned[...], right[...])
    split_rows(scal, acc, send, keep)


def up_call(scal, left, right, n_dp):
    rows = D // n_dp
    half = n_dp // 2
    cols = 768
    shape = jax.ShapeDtypeStruct((half, rows, FF), BF16)
    spec = pl.BlockSpec((half, rows, cols), lambda i: (0, 0, i))
    return pl.pallas_call(
        up_kernel,
        name="grad_up",
        grid=(FF // cols,),
        out_shape=[shape, shape],
        in_specs=[SM, VM, pl.BlockSpec((TOK, cols), lambda i: (0, i))],
        out_specs=[spec, spec],
        scratch_shapes=[pltpu.VMEM((D, TOK), BF16), pltpu.VMEM((D, cols), F32)],
        compiler_params=pltpu.CompilerParams(vmem_limit_bytes=40 << 20),
        cost_estimate=pl.CostEstimate(flops=2 * TOK * D * FF, bytes_accessed=10 << 20, transcendentals=0),
    )(scal, left.reshape(TOK, D), right.reshape(TOK, FF))


def attn_kernel(scal, normed, mnormed, gqkv, gml, send, keep, turned, acc):
    step = pl.program_id(0)

    @pl.when(step == 0)
    def _():
        turned[...] = normed[...].T

    @pl.when(step == 3)
    def _():
        turned[...] = mnormed[...].T

    @pl.when(step < 3)
    def _():
        acc[...] = dot_nn(turned[...], gqkv[...])

    @pl.when(step == 3)
    def _():
        acc[...] = dot_nn(turned[...], gml[...])

    split_rows(scal, acc, send, keep)


def attn_call(scal, normed, mnormed, gqkv, gml, n_dp):
    rows = D // n_dp
    half = n_dp // 2
    shape = jax.ShapeDtypeStruct((half, rows, 4 * D), BF16)
    spec = pl.BlockSpec((half, rows, D), lambda i: (0, 0, i))
    return pl.pallas_call(
        attn_kernel,
        name="grad_attn",
        grid=(4,),
        out_shape=[shape, shape],
        in_specs=[SM, VM, VM, pl.BlockSpec((TOK, D), lambda i: (0, jnp.minimum(i, 2))), VM],
        out_specs=[spec, spec],
        scratch_shapes=[pltpu.VMEM((D, TOK), BF16), pltpu.VMEM((D, D), F32)],
        compiler_params=pltpu.CompilerParams(vmem_limit_bytes=40 << 20),
        cost_estimate=pl.CostEstimate(flops=2 * TOK * D * 4 * D, bytes_accessed=14 << 20, transcendentals=0),
    )(
        scal,
        normed.reshape(TOK, D),
        mnormed.reshape(TOK, D),
        gqkv.reshape(TOK, 3 * D),
        gml.reshape(TOK, D),
    )


def halve(send, keep, n_dp, wide=BF16):
    me = lax.axis_index("dp")
    bit = 1
    while True:
        got = lax.ppermute(send, "dp", [(i, i ^ bit) for i in range(n_dp)])
        bit *= 2
        if bit == n_dp:
            return (keep[0].astype(F32) + got[0].astype(F32))
        mine = (me // bit) % 2
        pairs = (keep.shape[0] // 2, 2) + keep.shape[1:]
        keep, got = keep.reshape(pairs), got.reshape(pairs)

        def pick(which):
            a = lax.dynamic_index_in_dim(keep, which, 1, keepdims=False)
            b = lax.dynamic_index_in_dim(got, which, 1, keepdims=False)
            return (a.astype(F32) + b.astype(F32)).astype(wide)

        send, keep = pick(1 - mine), pick(mine)


def token_product(left, right):
    left, right = (t.reshape(TOK, t.shape[-1]) for t in (left, right))
    return lax.psum_scatter(dot_tn(left, right), "dp", scatter_dimension=0, tiled=True)


def shifted(x, by):
    length = lax.axis_size("section")
    pairs = [(i, i + by) for i in range(length) if 0 <= i + by < length]
    return lax.ppermute(x, "section", pairs)


def local(n_dp, inputs, out_cotangent, sequence_ids, *raw):
    wqk, wv, wout, wup, wdown, gains, shifts, fg, fs, pb, ub = (w[0] for w in raw)
    params = (wqk, wv, wout, wup, wdown, gains, shifts, fg[None], fs[None], pb, ub[None])
    sec = lax.axis_index("section")
    me = lax.axis_index("dp")
    inp = inputs.reshape(MICRO, ROWS, D)
    cot = out_cotangent.reshape(MICRO, ROWS, D)
    seq = sequence_ids.reshape(MICRO, 1, ROWS)

    def control(m0, m1):
        a0, a1 = int(m0 is not None), int(m1 is not None)
        return jnp.stack([jnp.where(sec == 0, a0, a1), jnp.where(sec == 0, m0 or 0, m1 or 0), sec]).astype(jnp.int32)

    def fwd(m0, m1, recv, fstate):
        return forward_call(control(m0, m1), inp, recv, seq, params, fstate)

    def bwd(m0, m1, recv, fstate, bstate):
        return backward_call(control(m0, m1), cot, recv, seq, params, fstate, bstate)

    none = inp[0]
    fs_, r0 = fwd(0, None, none, None)
    p0 = shifted(r0, 1)
    fs_, r1 = fwd(1, None, none, fs_)
    p1 = shifted(r1, 1)
    fs_, r2 = fwd(2, 0, p0, fs_)
    p2 = shifted(r2, 1)
    bs_, g0 = bwd(None, 0, none, fs_, None)
    q0 = shifted(g0, -1)
    fs_, _ = fwd(None, 1, p1, fs_)
    bs_, g1 = bwd(None, 1, none, fs_, bs_)
    q1 = shifted(g1, -1)
    fs_, _ = fwd(None, 2, p2, fs_)
    bs_, g2 = bwd(0, 2, q0, fs_, bs_)
    q2 = shifted(g2, -1)
    bs_, _ = bwd(1, None, q1, fs_, bs_)
    state = dict(zip([s[0] for s in F_STATE], fs_))
    core = jnp.stack([me % 2, sec]).astype(jnp.int32)
    blocks = (D // n_dp) % 16 == 0
    if blocks:
        s_down, k_down = down_call(core, state["hn"], cot, (q0, q1, q2), n_dp)
    bs_, _ = bwd(2, None, q2, fs_, bs_)
    state.update(zip(("dh", "gml", "gqkv", "igr", "vec", "vecf"), bs_))
    if blocks:
        s_up, k_up = up_call(core, state["ffn_in"], state["dh"], n_dp)
        s_att, k_att = attn_call(core, state["normed"], state["mnormed"], state["gqkv"], state["gml"], n_dp)
        g_down = halve(s_down, k_down, n_dp)
        g_up = halve(s_up, k_up, n_dp)
        g_att = halve(s_att, k_att, n_dp)
    else:
        gy = jnp.where(sec == 0, jnp.stack([q0, q1, q2]), cot)
        g_down = token_product(state["hn"], gy)
        g_up = token_product(state["ffn_in"], state["dh"])
        g_att = jnp.concatenate(
            [token_product(state["normed"], state["gqkv"]), token_product(state["mnormed"], state["gml"])], axis=1
        )
    vec = jnp.sum(state["vec"], axis=0)[:10].reshape(10, n_dp, D // n_dp)
    vecf = jnp.sum(state["vecf"], axis=0)[:3].reshape(3, n_dp, FF // n_dp)
    vecs = jnp.concatenate([vec.transpose(1, 0, 2).reshape(n_dp, -1), vecf.transpose(1, 0, 2).reshape(n_dp, -1)], axis=1)
    vecs = vecs.reshape(n_dp // 2, 2, 1, -1)
    s_vec = lax.dynamic_index_in_dim(vecs, 1 - me % 2, 1, keepdims=False)
    k_vec = lax.dynamic_index_in_dim(vecs, me % 2, 1, keepdims=False)
    g_vec = halve(s_vec, k_vec, n_dp, F32)[0]
    n1, n2 = D // n_dp, FF // n_dp
    va = g_vec[: 10 * n1].reshape(10, n1)
    vb = g_vec[10 * n1 :].reshape(3, n2)
    rows = MICRO * ROWS
    return (
        state["louts"].reshape(1, rows, D),
        state["igr"].reshape(1, rows, D),
        g_att[None, :, : 2 * D],
        g_att[None, :, 2 * D : 3 * D],
        g_att[None, :, 3 * D :],
        g_up[None],
        g_down[None],
        va[0:3][None],
        va[3:6][None],
        vb[0:1],
        vb[1:2],
        va[6:10][None],
        vb[2:3],
    )


def solution(mesh):
    in_specs = (
        P("dp", None),
        P("dp", None),
        P("dp", None),
        P("section", None, None),
        P("section", None, None),
        P("section", None, None),
        P("section", None, None),
        P("section", None, None),
        P("section", None, None),
        P("section", None, None),
        P("section", None),
        P("section", None),
        P("section", None, None),
        P("section", None),
    )
    out_specs = (
        P("section", "dp", None),
        P("section", "dp", None),
        P("section", "dp", None),
        P("section", "dp", None),
        P("section", "dp", None),
        P("section", "dp", None),
        P("section", "dp", None),
        P("section", None, "dp"),
        P("section", None, "dp"),
        P("section", "dp"),
        P("section", "dp"),
        P("section", None, "dp"),
        P("section", "dp"),
    )
    body = functools.partial(local, mesh.shape["dp"])
    return jax.shard_map(body, mesh=mesh, in_specs=in_specs, out_specs=out_specs, check_vma=False)
```

```python
import functools

import jax
import jax.numpy as jnp
from jax import lax
from jax.experimental import pallas as pl
from jax.experimental.pallas import tpu as pltpu
from jax.sharding import PartitionSpec as P

D = 768
HEADS = 12
HEAD_DIM = 64
FF = 3072
ROWS = 256
MICRO = 3
EPS = 1e-05
MASKED = -1e30
CH = 512
N_CH = FF // CH
UNROLL_ATT_F = 3
UNROLL_ATT_B = 2
UNROLL_UP = 2
UNROLL_DOWN = 2
UNROLL_B1 = 2
UNROLL_B2 = 2
VMEM_ALL = 63 << 20
PAIRS = HEADS // 2
F32 = jnp.float32
BF16 = jnp.bfloat16
ANY = pl.BlockSpec(memory_space=pl.ANY)
VM = pl.BlockSpec(memory_space=pltpu.VMEM)
SM = pl.BlockSpec(memory_space=pltpu.SMEM)


def dot_nn(a, b):
    return lax.dot_general(a, b, (((1,), (0,)), ((), ())), preferred_element_type=F32)


def dot_nt(a, b):
    return lax.dot_general(a, b, (((1,), (1,)), ((), ())), preferred_element_type=F32)


def dot_tn(a, b):
    return lax.dot_general(a, b, (((0,), (0,)), ((), ())), preferred_element_type=F32)


def center_spread(v):
    c = v - jnp.mean(v, axis=-1, keepdims=True)
    r = lax.rsqrt(jnp.mean(c * c, axis=-1, keepdims=True) + EPS)
    return c, r


def norm(v, gain, shift):
    c, r = center_spread(v)
    return c * r * gain + shift


def norm_back(grad, v, gain):
    c, r = center_spread(v)
    x = c * r
    h = grad * gain
    back = r * (h - jnp.mean(h, axis=-1, keepdims=True) - x * jnp.mean(h * x, axis=-1, keepdims=True))
    return back, colsum(grad * x), colsum(grad)


def colsum(v):
    return jnp.sum(v, axis=0, keepdims=True)


def lane_fold(v):
    total = v[:, :128]
    for k in range(1, v.shape[1] // 128):
        total = total + v[:, k * 128 : (k + 1) * 128]
    return total


def same_bias(seq_row):
    rows = jnp.broadcast_to(seq_row.astype(F32), (ROWS, ROWS))
    return jnp.where(rows == rows.T, 0.0, MASKED)


def aligned(i, size):
    return pl.ds(pl.multiple_of(i * size, size), size)


SAVED = (
    ("src", D, BF16),
    ("qkv", 3 * D, BF16),
    ("mixed", D, BF16),
    ("middle", D, BF16),
    ("xh", FF, BF16),
    ("gp", FF, BF16),
    ("rst", 128, F32),
)
F_OUT = (
    ("normed", D, BF16),
    ("mnormed", D, BF16),
    ("ffn_in", D, BF16),
    ("hn", FF, BF16),
    ("louts", D, BF16),
)
B_OUT = (
    ("dh", FF, BF16),
    ("gml", D, BF16),
    ("gqkv", 3 * D, BF16),
    ("igr", D, BF16),
    ("vec", D, F32),
    ("vecf", FF, F32),
)
STATE = SAVED + F_OUT + B_OUT
SMALL = (("gains", 3, D), ("shifts", 3, D), ("fg", 1, FF), ("fs", 1, FF), ("pb", 4, D), ("ub", 1, FF))
WEIGHTS = (("wqk", D, 2 * D), ("wv", D, D), ("wout", D, D), ("wup", D, FF), ("wdown", FF, D))


def rows_of(name):
    return {"vec": 16, "vecf": 8}.get(name, ROWS)


def inner_forward(v, cp, wait):
    normed_v, qkv, mid, act = v["normed"], v["qkv"], v["mid"], v["act"]
    gains, shifts, fg, fs, pb, ub = (v[n[0]] for n in SMALL)
    u = v["src"][...].astype(F32)
    normed_v[...] = norm(u, gains[0:1], shifts[0:1]).astype(BF16)
    cp.save("normed")
    wait("wqk", "wv")
    cp.load_late("wout", "wup")

    def project(i, _):
        at = aligned(i, 768)
        x = dot_nn(normed_v[...], v["wqkv"][:, at]) + v["qkvb"][0:1, at]
        qkv[:, at] = (x * jnp.where(i == 0, 0.125, 1.0)).astype(BF16)
        return 0

    lax.fori_loop(0, 3, project, 0)
    cp.save_kept("qkv")
    low = lax.broadcasted_iota(jnp.int32, (ROWS, 128), 1) < HEAD_DIM

    def pair(j, _):
        q2 = qkv[:, aligned(j, 128)]
        k2 = qkv[:, aligned(j + PAIRS, 128)]
        v2 = qkv[:, aligned(j + 2 * PAIRS, 128)]
        zero = jnp.zeros_like(k2)
        one = jnp.ones_like(v2)
        sums = []
        for first in (True, False):
            kh = jnp.where(low, k2, zero) if first else jnp.where(low, zero, k2)
            vh = jnp.where(low, v2, one) if first else jnp.where(low, one, v2)
            scores = dot_nt(q2, kh) + v["bias"][...]
            lifted = jnp.exp(scores - jnp.max(scores, axis=-1, keepdims=True)).astype(BF16)
            sums.append(dot_nn(lifted, vh))
        top = jnp.where(low, sums[0], sums[1])
        den = pltpu.roll(jnp.where(low, sums[1], sums[0]), 64, 1)
        mid[:, aligned(j, 128)] = top / den
        return 0

    lax.fori_loop(0, PAIRS, pair, 0, unroll=UNROLL_ATT_F)
    cp.load_late("wdown")
    mixed = mid[...]
    v["mixed"][...] = mixed.astype(BF16)
    cp.save_kept("mixed")
    mnormed = norm(mixed, gains[1:2], shifts[1:2]).astype(BF16)
    v["mnormed"][...] = mnormed
    cp.save("mnormed")
    wait("wout")
    middle = v["src"][...].astype(F32) + dot_nn(mnormed, v["wout"][...]) + pb[2:3]
    mid[...] = middle
    v["middle"][...] = middle.astype(BF16)
    cp.save_kept("middle")
    cp.save_kept("src")
    v["ffn_in"][...] = norm(middle, gains[2:3], shifts[2:3]).astype(BF16)
    cp.save("ffn_in")
    wait("wup")

    def up(i, total):
        at = aligned(i, CH)
        h = dot_nn(v["ffn_in"][...], v["wup"][:, at]) + ub[:, at]
        cdf = 0.5 + 0.5 * lax.erf(h * 0.7071067811865476)
        a = h * cdf
        act[:, at] = a
        pdf = jnp.exp2(h * h * -0.7213475204444817 - 1.3257480647361594)
        v["gp"][:, at] = (cdf + h * pdf).astype(BF16)
        return total + lane_fold(a)

    total = lax.fori_loop(0, N_CH, up, jnp.zeros((ROWS, 128), F32), unroll=UNROLL_UP)
    cp.save_kept("gp")
    mean = jnp.sum(total, axis=-1, keepdims=True) * (1.0 / FF)

    def spread(i, total):
        c = act[:, aligned(i, CH)] - mean
        return total + lane_fold(c * c)

    total = lax.fori_loop(0, N_CH, spread, jnp.zeros((ROWS, 128), F32))
    r = lax.rsqrt(jnp.sum(total, axis=-1, keepdims=True) * (1.0 / FF) + EPS)
    v["rst"][...] = jnp.broadcast_to(r, (ROWS, 128))
    cp.save_kept("rst")
    wait("wdown")
    v["acc"][...] = mid[...] + pb[3:4]

    def down(i, _):
        at = aligned(i, CH)
        x = (act[:, at] - mean) * r
        v["xh"][:, at] = x.astype(BF16)
        hn = (x * fg[:, at] + fs[:, at]).astype(BF16)
        v["hn"][:, at] = hn
        v["acc"][...] += dot_nn(hn, v["wdown"][at, :])
        return 0

    lax.fori_loop(0, N_CH, down, 0, unroll=UNROLL_DOWN)
    v["louts"][...] = v["acc"][...].astype(BF16)
    cp.save("louts")
    cp.save("res")
    cp.save("hn")
    cp.save_kept("xh")


def inner_backward(v, cp, wait, ready):
    gains, fg = v["gains"], v["fg"]
    act, acc, mid, gy_b, xh, gp, qkv, gqkv = (v[n] for n in ("act", "acc", "mid", "gy", "xh", "gp", "qkv", "gqkv"))
    vec, vecf = v["vec"], v["vecf"]
    vec[9:10] = colsum(gy_b[...].astype(F32))
    wait("wdown")
    ready("xh")

    def first(i, totals):
        at = aligned(i, CH)
        g = dot_nt(gy_b[...], v["wdown"][at, :])
        x = xh[:, at].astype(F32)
        gx = g * x
        vecf[0:1, at] = colsum(gx)
        vecf[1:2, at] = colsum(g)
        h = g * fg[:, at]
        act[:, at] = h
        return totals[0] + lane_fold(h), totals[1] + lane_fold(h * x)

    zeros = jnp.zeros((ROWS, 128), F32)
    t1, t2 = lax.fori_loop(0, N_CH, first, (zeros, zeros), unroll=UNROLL_B1)
    m1 = jnp.sum(t1, axis=-1, keepdims=True) * (1.0 / FF)
    m2 = jnp.sum(t2, axis=-1, keepdims=True) * (1.0 / FF)
    ready("gp", "rst")
    wait("wup")
    r = v["rst"][:, 0:1]
    acc[...] = jnp.zeros_like(acc)

    def second(i, _):
        at = aligned(i, CH)
        x = xh[:, at].astype(F32)
        d = (act[:, at] - m1 - x * m2) * r * gp[:, at].astype(F32)
        vecf[2:3, at] = colsum(d)
        low_d = d.astype(BF16)
        v["dh"][:, at] = low_d
        acc[...] += dot_nt(low_d, v["wup"][:, at])
        return 0

    lax.fori_loop(0, N_CH, second, 0, unroll=UNROLL_B2)
    cp.save("dh")
    cp.save("vecf")
    ready("middle")
    back, v_gain, v_shift = norm_back(acc[...], v["middle"][...].astype(F32), gains[2:3])
    vec[2:3] = v_gain
    vec[5:6] = v_shift
    gm = gy_b[...].astype(F32) + back
    mid[...] = gm
    gml_v = gm.astype(BF16)
    v["gml"][...] = gml_v
    cp.save("gml")
    vec[8:9] = colsum(gm)
    wait("wout")
    ready("mixed")
    back, v_gain, v_shift = norm_back(dot_nt(gml_v, v["wout"][...]), v["mixed"][...].astype(F32), gains[1:2])
    vec[1:2] = v_gain
    vec[4:5] = v_shift
    v["gmix"][...] = back.astype(BF16)
    ready("qkv")
    low = lax.broadcasted_iota(jnp.int32, (ROWS, 128), 1) < HEAD_DIM

    def pair(j, _):
        q2 = qkv[:, aligned(j, 128)]
        k2 = qkv[:, aligned(j + PAIRS, 128)]
        v2 = qkv[:, aligned(j + 2 * PAIRS, 128)]
        g2 = v["gmix"][:, aligned(j, 128)]
        zero = jnp.zeros_like(k2)
        gq = gk = gv = None
        for head in range(2):

            def half(t):
                return jnp.where(low, t, zero) if head == 0 else jnp.where(low, zero, t)

            kh, vh, qh, gh = half(k2), half(v2), half(q2), half(g2)
            st = dot_nt(kh, q2) + v["bias"][...]
            e = jnp.exp(st - jnp.max(st, axis=0, keepdims=True))
            p = e * (1.0 / jnp.sum(e, axis=0, keepdims=True))
            gp_t = dot_nt(vh, g2)
            inner = jnp.sum(p * gp_t, axis=0, keepdims=True)
            gs = (p * (gp_t - inner)).astype(BF16)
            a = dot_nn(p.astype(BF16), gh)
            b = dot_nn(gs, qh)
            c = dot_tn(gs, kh * 0.125)
            gv = a if gv is None else gv + a
            gk = b if gk is None else gk + b
            gq = c if gq is None else gq + c
        gqkv[:, aligned(j, 128)] = gq.astype(BF16)
        gqkv[:, aligned(j + PAIRS, 128)] = gk.astype(BF16)
        gqkv[:, aligned(j + 2 * PAIRS, 128)] = gv.astype(BF16)
        vec[6:7, aligned(j, 128)] = colsum(gq)
        vec[7:8, aligned(j, 128)] = colsum(gv)
        return 0

    lax.fori_loop(0, PAIRS, pair, 0, unroll=UNROLL_ATT_B)
    cp.save("gqkv")
    wait("wqk", "wv")
    ready("src")

    def back_chunk(i, _):
        at = aligned(i, 768)
        acc[...] += dot_nt(gqkv[:, at], v["wqkv"][:, at])
        return 0

    acc[...] = jnp.zeros_like(acc)
    lax.fori_loop(0, 3, back_chunk, 0)
    back, v_gain, v_shift = norm_back(acc[...], v["src"][...].astype(F32), gains[0:1])
    vec[0:1] = v_gain
    vec[3:4] = v_shift
    v["igr"][...] = (mid[...] + back).astype(BF16)
    cp.save("send")
    cp.save("igr")
    cp.save("vec")


class Traffic:
    def __init__(self, v, hbm, sems, mb, both):
        self.v, self.hbm, self.sems, self.mb, self.both = v, hbm, sems, mb, both
        self.at = {}
        self.kept = []
        self.late = True

    def sem(self, key):
        return self.sems.at[self.at.setdefault(key, len(self.at))]

    def weight(self, name):
        dst = self.v[name] if name in ("wout", "wup", "wdown") else None
        if name == "wqk":
            dst = self.v["wqkv"].at[:, pl.ds(0, 2 * D)]
        if name == "wv":
            dst = self.v["wqkv"].at[:, pl.ds(2 * D, D)]
        return pltpu.make_async_copy(self.hbm[name], dst, self.sem(name))

    def load_late(self, *names):
        for n in names:
            self.weight(n).start()

    def out(self, name):
        source = {"res": "louts", "send": "igr"}.get(name, name)
        dst = self.hbm[name] if name in ("res", "send") else self.hbm["o_" + name].at[self.mb]
        return pltpu.make_async_copy(self.v[source], dst, self.sem("o_" + name))

    def save(self, name):
        copy = self.out(name)
        copy.start()
        self.kept.append((name, False))

    def save_kept(self, name):
        copy = self.out(name)
        self.kept.append((name, True))

        @pl.when(jnp.logical_not(self.both))
        def _():
            copy.start()

    def finish(self):
        for name, conditional in self.kept:
            if conditional:

                @pl.when(jnp.logical_not(self.both))
                def _(name=name):
                    self.out(name).wait()
            else:
                self.out(name).wait()
        self.kept = []


def layer_kernel(has_f, has_b, n_alias, names_in, *refs):
    n_in = 5 + len(SMALL) + len(WEIGHTS)
    scal, inp_all, f_recv, cot_all, b_recv = refs[:5]
    hbm = dict(zip([n[0] for n in SMALL + WEIGHTS], refs[5:n_in]))
    k = n_in
    ins = dict(zip(names_in, refs[k : k + len(names_in)]))
    seq_h = refs[k + len(names_in)]
    k += len(names_in) + 1 + n_alias
    outs = kernel_outs(has_f, has_b)
    for name in outs:
        hbm["o_" + name if name not in ("res", "send") else name] = refs[k]
        k += 1
    v = dict(zip([n for n, _, _ in kernel_scratch(has_f, has_b)], refs[k:]))
    sems = refs[-1]
    do_f, do_b, mb, sec = scal[0] == 1, scal[1] == 1, scal[2], scal[4]
    only_b = jnp.logical_and(do_b, jnp.logical_not(do_f))

    @pl.when(jnp.logical_or(do_f, do_b))
    def _():
        cp = Traffic(v, hbm, sems, mb, do_b)
        smalls = [pltpu.make_async_copy(hbm[n], v[n], cp.sem(n)) for n, _, _ in SMALL]
        seq_copy = pltpu.make_async_copy(seq_h.at[mb], v["seq"], cp.sem("seq"))
        first_in = pltpu.make_async_copy(f_recv, v["src"], cp.sem("in")) if has_f else None
        gy_in = pltpu.make_async_copy(b_recv, v["gy"], cp.sem("gy")) if has_b else None

        def pick(copy, other, own):
            @pl.when(own)
            def _():
                other.start()

            @pl.when(jnp.logical_not(own))
            def _():
                copy.start()

        loads = {n: pltpu.make_async_copy(ins[n].at[mb], v[n], cp.sem("i_" + n)) for n in names_in} if has_b else {}
        if has_f:

            @pl.when(do_f)
            def _():
                pick(first_in, pltpu.make_async_copy(inp_all.at[mb], v["src"], cp.sem("in")), sec == 0)
                cp.load_late("wqk", "wv")

        for c in smalls:
            c.start()
        seq_copy.start()
        if has_b:

            @pl.when(do_b)
            def _():
                pick(gy_in, pltpu.make_async_copy(cot_all.at[mb], v["gy"], cp.sem("gy")), sec != 0)

            @pl.when(only_b)
            def _():
                cp.load_late("wdown")
                for n in ("xh", "gp", "rst"):
                    loads[n].start()
                cp.load_late("wup")
                for n in ("middle", "mixed", "qkv", "src"):
                    loads[n].start()
                cp.load_late("wout", "wqk", "wv")

        seq_copy.wait()
        v["bias"][...] = same_bias(v["seq"][...])
        for c in smalls:
            c.wait()
        if has_f:

            @pl.when(do_f)
            def _():
                v["qkvb"][:, 0:D] = v["pb"][0:1]
                v["qkvb"][:, D : 2 * D] = jnp.zeros((1, D), F32)
                v["qkvb"][:, 2 * D :] = v["pb"][1:2]
                first_in.wait()

                def wait(*names):
                    for n in names:
                        cp.weight(n).wait()

                inner_forward(v, cp, wait)
                if not has_b:
                    cp.finish()

        if has_b:

            @pl.when(do_b)
            def _():
                gy_in.wait()

                def wait(*names):
                    @pl.when(only_b)
                    def _():
                        for n in names:
                            cp.weight(n).wait()

                def ready(*names):
                    @pl.when(only_b)
                    def _():
                        for n in names:
                            loads[n].wait()

                back = Traffic(v, hbm, sems, mb, do_b)
                back.at = cp.at
                inner_backward(v, back, wait, ready)
                back.finish()

            if has_f:

                @pl.when(do_f)
                def _():
                    cp.finish()


def kernel_outs(has_f, has_b):
    names = []
    if has_f:
        names += [n for n, _, _ in SAVED + F_OUT] + ["res"]
    if has_b:
        names += [n for n, _, _ in B_OUT] + ["send"]
    return names


def kernel_scratch(has_f, has_b):
    out = [(n, (r, c), F32) for n, r, c in SMALL]
    out += [("wqkv", (D, 3 * D), BF16)]
    out += [(n, (r, c), BF16) for n, r, c in WEIGHTS[2:]]
    out += [(n, (ROWS, c), t) for n, c, t in SAVED]
    if has_f:
        out += [(n, (ROWS, c), t) for n, c, t in F_OUT] + [("qkvb", (1, 3 * D), F32)]
    if has_b:
        out += [(n, (rows_of(n), c), t) for n, c, t in B_OUT]
        out += [("gy", (ROWS, D), BF16), ("gmix", (ROWS, D), BF16)]
    out += [("seq", (1, ROWS), jnp.int32), ("bias", (ROWS, ROWS), F32)]
    out += [("act", (ROWS, FF), F32), ("acc", (ROWS, D), F32), ("mid", (ROWS, D), F32)]
    return out


def layer_call(scal, has_f, has_b, inp, f_recv, cot, b_recv, seq, params, state):
    wqk, wv, wout, wup, wdown, gains, shifts, fg, fs, pb, ub = params
    names_in = tuple(n for n, _, _ in SAVED) if has_b else ()
    outs = kernel_outs(has_f, has_b)
    alias = [n for n in outs if n in state]
    shapes = {n: (rows_of(n), c, t) for n, c, t in STATE}
    out_shape = []
    for n in outs:
        if n in ("res", "send"):
            out_shape.append(jax.ShapeDtypeStruct((ROWS, D), BF16))
        else:
            r, c, t = shapes[n]
            out_shape.append(jax.ShapeDtypeStruct((MICRO, r, c), t))
    separate = () if has_f else names_in
    operands = [scal, inp, f_recv, cot, b_recv, gains, shifts, fg, fs, pb, ub, wqk, wv, wout, wup, wdown]
    operands += [state[n] for n in separate] + [seq]
    base = len(operands)
    operands += [state[n] for n in alias]
    scratch = kernel_scratch(has_f, has_b)

    def body(*refs):
        if has_f and has_b:
            at = base + len(alias)
            by_name = dict(zip(outs, refs[at : at + len(outs)]))
            refs = refs[: base - 1] + tuple(by_name[n] for n in names_in) + refs[base - 1 :]
        layer_kernel(has_f, has_b, len(alias), names_in, *refs)

    got = pl.pallas_call(
        body,
        name="layer_" + "f" * has_f + "b" * has_b,
        out_shape=out_shape,
        in_specs=[SM] + [ANY] * (len(operands) - 1),
        out_specs=[ANY] * len(outs),
        scratch_shapes=[pltpu.VMEM(s, t) for _, s, t in scratch] + [pltpu.SemaphoreType.DMA((48,))],
        input_output_aliases={base + i: outs.index(n) for i, n in enumerate(alias)},
        compiler_params=pltpu.CompilerParams(vmem_limit_bytes=VMEM_ALL),
        cost_estimate=pl.CostEstimate(flops=4 * 10**9 * (has_f + has_b), bytes_accessed=24 << 20, transcendentals=10**6),
    )(*operands)
    got = dict(zip(outs, got))
    state = dict(state)
    state.update({n: a for n, a in got.items() if n not in ("res", "send")})
    return got.get("res"), got.get("send"), state


TOK = MICRO * ROWS


def down_kernel(scal, hn, cot, q0, q1, q2, send, keep, gy, acc, sems):
    @pl.when(pl.program_id(0) == 0)
    def _():
        @pl.when(scal[1] == 0)
        def _():
            copies = [
                pltpu.make_async_copy(q, gy.at[pl.ds(i * ROWS, ROWS)], sems.at[i])
                for i, q in enumerate((q0, q1, q2))
            ]
            for c in copies:
                c.start()
            for c in copies:
                c.wait()

        @pl.when(scal[1] != 0)
        def _():
            c = pltpu.make_async_copy(cot, gy, sems.at[0])
            c.start()
            c.wait()

    half = acc.shape[0] // 2
    acc[...] = dot_tn(hn[...], gy[...])
    core = scal[0]
    send[0] = acc[pl.ds(pl.multiple_of((1 - core) * half, half), half), :].astype(BF16)
    keep[0] = acc[pl.ds(pl.multiple_of(core * half, half), half), :].astype(BF16)


def down_call(scal, hn, cot, qs, n_dp):
    rows = FF // n_dp
    half = n_dp // 2
    shape = jax.ShapeDtypeStruct((half, rows, D), BF16)
    spec = pl.BlockSpec((1, rows, D), lambda i: (i, 0, 0))
    return pl.pallas_call(
        down_kernel,
        name="grad_down",
        grid=(half,),
        out_shape=[shape, shape],
        in_specs=[SM, pl.BlockSpec((TOK, 2 * rows), lambda i: (0, i)), ANY, ANY, ANY, ANY],
        out_specs=[spec, spec],
        scratch_shapes=[
            pltpu.VMEM((TOK, D), BF16),
            pltpu.VMEM((2 * rows, D), F32),
            pltpu.SemaphoreType.DMA((3,)),
        ],
        compiler_params=pltpu.CompilerParams(vmem_limit_bytes=VMEM_ALL),
        cost_estimate=pl.CostEstimate(flops=2 * TOK * D * FF, bytes_accessed=10 << 20, transcendentals=0),
    )(scal, hn.reshape(TOK, FF), cot.reshape(TOK, D), *qs)


def split_rows(scal, acc, send, keep):
    half, rows = send.shape[0], send.shape[1]
    core = scal[0]
    for j in range(half):
        send[j] = acc[pl.ds(pl.multiple_of((2 * j + 1 - core) * rows, rows), rows), :].astype(BF16)
        keep[j] = acc[pl.ds(pl.multiple_of((2 * j + core) * rows, rows), rows), :].astype(BF16)


def up_kernel(scal, left, right, send, keep, turned, acc):
    @pl.when(pl.program_id(0) == 0)
    def _():
        turned[...] = left[...].T

    acc[...] = dot_nn(turned[...], right[...])
    split_rows(scal, acc, send, keep)


def up_call(scal, left, right, n_dp):
    rows = D // n_dp
    half = n_dp // 2
    cols = 768
    shape = jax.ShapeDtypeStruct((half, rows, FF), BF16)
    spec = pl.BlockSpec((half, rows, cols), lambda i: (0, 0, i))
    return pl.pallas_call(
        up_kernel,
        name="grad_up",
        grid=(FF // cols,),
        out_shape=[shape, shape],
        in_specs=[SM, VM, pl.BlockSpec((TOK, cols), lambda i: (0, i))],
        out_specs=[spec, spec],
        scratch_shapes=[pltpu.VMEM((D, TOK), BF16), pltpu.VMEM((D, cols), F32)],
        compiler_params=pltpu.CompilerParams(vmem_limit_bytes=VMEM_ALL),
        cost_estimate=pl.CostEstimate(flops=2 * TOK * D * FF, bytes_accessed=10 << 20, transcendentals=0),
    )(scal, left.reshape(TOK, D), right.reshape(TOK, FF))


def attn_kernel(scal, normed, mnormed, gqkv, gml, send, keep, turned, acc):
    step = pl.program_id(0)

    @pl.when(step == 0)
    def _():
        turned[...] = normed[...].T

    @pl.when(step == 3)
    def _():
        turned[...] = mnormed[...].T

    @pl.when(step < 3)
    def _():
        acc[...] = dot_nn(turned[...], gqkv[...])

    @pl.when(step == 3)
    def _():
        acc[...] = dot_nn(turned[...], gml[...])

    split_rows(scal, acc, send, keep)


def attn_call(scal, normed, mnormed, gqkv, gml, n_dp):
    rows = D // n_dp
    half = n_dp // 2
    shape = jax.ShapeDtypeStruct((half, rows, 4 * D), BF16)
    spec = pl.BlockSpec((half, rows, D), lambda i: (0, 0, i))
    return pl.pallas_call(
        attn_kernel,
        name="grad_attn",
        grid=(4,),
        out_shape=[shape, shape],
        in_specs=[SM, VM, VM, pl.BlockSpec((TOK, D), lambda i: (0, jnp.minimum(i, 2))), VM],
        out_specs=[spec, spec],
        scratch_shapes=[pltpu.VMEM((D, TOK), BF16), pltpu.VMEM((D, D), F32)],
        compiler_params=pltpu.CompilerParams(vmem_limit_bytes=VMEM_ALL),
        cost_estimate=pl.CostEstimate(flops=2 * TOK * D * 4 * D, bytes_accessed=14 << 20, transcendentals=0),
    )(
        scal,
        normed.reshape(TOK, D),
        mnormed.reshape(TOK, D),
        gqkv.reshape(TOK, 3 * D),
        gml.reshape(TOK, D),
    )


def halve(send, keep, n_dp, wide=BF16):
    me = lax.axis_index("dp")
    bit = 1
    while True:
        got = lax.ppermute(send, "dp", [(i, i ^ bit) for i in range(n_dp)])
        bit *= 2
        if bit == n_dp:
            return (keep[0].astype(F32) + got[0].astype(F32))
        mine = (me // bit) % 2
        pairs = (keep.shape[0] // 2, 2) + keep.shape[1:]
        keep, got = keep.reshape(pairs), got.reshape(pairs)

        def pick(which):
            a = lax.dynamic_index_in_dim(keep, which, 1, keepdims=False)
            b = lax.dynamic_index_in_dim(got, which, 1, keepdims=False)
            return (a.astype(F32) + b.astype(F32)).astype(wide)

        send, keep = pick(1 - mine), pick(mine)


def token_product(left, right):
    left, right = (t.reshape(TOK, t.shape[-1]) for t in (left, right))
    return lax.psum_scatter(dot_tn(left, right), "dp", scatter_dimension=0, tiled=True)


def shifted(x, by):
    length = lax.axis_size("section")
    pairs = [(i, i + by) for i in range(length) if 0 <= i + by < length]
    return lax.ppermute(x, "section", pairs)


def local(n_dp, inputs, out_cotangent, sequence_ids, *raw):
    wqk, wv, wout, wup, wdown, gains, shifts, fg, fs, pb, ub = (w[0] for w in raw)
    params = (wqk, wv, wout, wup, wdown, gains, shifts, fg[None], fs[None], pb, ub[None])
    sec = lax.axis_index("section")
    me = lax.axis_index("dp")
    inp = inputs.reshape(MICRO, ROWS, D)
    cot = out_cotangent.reshape(MICRO, ROWS, D)
    seq = sequence_ids.reshape(MICRO, 1, ROWS)

    def control(f0, b0, f1, b1):
        def code(f, b):
            mb = next((m for m in (f, b) if m is not None), 0)
            return jnp.array([f is not None, b is not None, mb, 0, 0], jnp.int32)

        return jnp.where(sec == 0, code(f0, b0), code(f1, b1)).at[4].set(sec)

    none = inp[0]
    state = {}

    def run(f0, b0, f1, b1, f_recv=none, b_recv=none):
        nonlocal state
        has_f, has_b = f0 is not None or f1 is not None, b0 is not None or b1 is not None
        scal = control(f0, b0, f1, b1)
        res, send, state = layer_call(scal, has_f, has_b, inp, f_recv, cot, b_recv, seq, params, state)
        return res, send

    r0, _ = run(0, None, None, None)
    p0 = shifted(r0, 1)
    r1, _ = run(1, None, None, None)
    p1 = shifted(r1, 1)
    r2, g0 = run(2, None, 0, 0, f_recv=p0)
    p2 = shifted(r2, 1)
    q0 = shifted(g0, -1)
    _, g1 = run(None, None, 1, 1, f_recv=p1)
    q1 = shifted(g1, -1)
    _, g2 = run(None, 0, 2, 2, f_recv=p2, b_recv=q0)
    q2 = shifted(g2, -1)
    run(None, 1, None, None, b_recv=q1)
    core = jnp.stack([me % 2, sec]).astype(jnp.int32)
    blocks = (D // n_dp) % 16 == 0
    if blocks:
        s_down, k_down = down_call(core, state["hn"], cot, (q0, q1, q2), n_dp)
    run(None, 2, None, None, b_recv=q2)
    if blocks:
        s_up, k_up = up_call(core, state["ffn_in"], state["dh"], n_dp)
        s_att, k_att = attn_call(core, state["normed"], state["mnormed"], state["gqkv"], state["gml"], n_dp)
        g_down = halve(s_down, k_down, n_dp)
        g_up = halve(s_up, k_up, n_dp)
        g_att = halve(s_att, k_att, n_dp)
    else:
        gy = jnp.where(sec == 0, jnp.stack([q0, q1, q2]), cot)
        g_down = token_product(state["hn"], gy)
        g_up = token_product(state["ffn_in"], state["dh"])
        g_att = jnp.concatenate(
            [token_product(state["normed"], state["gqkv"]), token_product(state["mnormed"], state["gml"])], axis=1
        )
    vec = jnp.sum(state["vec"], axis=0)[:10].reshape(10, n_dp, D // n_dp)
    vecf = jnp.sum(state["vecf"], axis=0)[:3].reshape(3, n_dp, FF // n_dp)
    vecs = jnp.concatenate([vec.transpose(1, 0, 2).reshape(n_dp, -1), vecf.transpose(1, 0, 2).reshape(n_dp, -1)], axis=1)
    vecs = vecs.reshape(n_dp // 2, 2, 1, -1)
    s_vec = lax.dynamic_index_in_dim(vecs, 1 - me % 2, 1, keepdims=False)
    k_vec = lax.dynamic_index_in_dim(vecs, me % 2, 1, keepdims=False)
    g_vec = halve(s_vec, k_vec, n_dp, F32)[0]
    n1, n2 = D // n_dp, FF // n_dp
    va = g_vec[: 10 * n1].reshape(10, n1)
    vb = g_vec[10 * n1 :].reshape(3, n2)
    rows = MICRO * ROWS
    return (
        state["louts"].reshape(1, rows, D),
        state["igr"].reshape(1, rows, D),
        g_att[None, :, : 2 * D],
        g_att[None, :, 2 * D : 3 * D],
        g_att[None, :, 3 * D :],
        g_up[None],
        g_down[None],
        va[0:3][None],
        va[3:6][None],
        vb[0:1],
        vb[1:2],
        va[6:10][None],
        vb[2:3],
    )


def solution(mesh):
    in_specs = (
        P("dp", None),
        P("dp", None),
        P("dp", None),
        P("section", None, None),
        P("section", None, None),
        P("section", None, None),
        P("section", None, None),
        P("section", None, None),
        P("section", None, None),
        P("section", None, None),
        P("section", None),
        P("section", None),
        P("section", None, None),
        P("section", None),
    )
    out_specs = (
        P("section", "dp", None),
        P("section", "dp", None),
        P("section", "dp", None),
        P("section", "dp", None),
        P("section", "dp", None),
        P("section", "dp", None),
        P("section", "dp", None),
        P("section", None, "dp"),
        P("section", None, "dp"),
        P("section", "dp"),
        P("section", "dp"),
        P("section", None, "dp"),
        P("section", "dp"),
    )
    body = functools.partial(local, mesh.shape["dp"])
    return jax.shard_map(body, mesh=mesh, in_specs=in_specs, out_specs=out_specs, check_vma=False)
```

```python
import functools

import jax
import jax.numpy as jnp
from jax import lax
from jax.experimental import pallas as pl
from jax.experimental.pallas import tpu as pltpu
from jax.sharding import PartitionSpec as P

D = 768
HEADS = 12
HEAD_DIM = 64
FF = 3072
ROWS = 256
MICRO = 3
EPS = 1e-05
MASKED = -1e30
CH = 512
N_CH = FF // CH
UNROLL_ATT_F = 3
UNROLL_ATT_B = 2
UNROLL_UP = 2
UNROLL_DOWN = 2
UNROLL_B1 = 2
UNROLL_B2 = 2
VMEM_ALL = 63 << 20
LIGHT = pl.CostEstimate(flops=1000, bytes_accessed=1000, transcendentals=0)
STEPS = 7
PAIRS = HEADS // 2
F32 = jnp.float32
BF16 = jnp.bfloat16
ANY = pl.BlockSpec(memory_space=pl.ANY)
VM = pl.BlockSpec(memory_space=pltpu.VMEM)
SM = pl.BlockSpec(memory_space=pltpu.SMEM)


def dot_nn(a, b):
    return lax.dot_general(a, b, (((1,), (0,)), ((), ())), preferred_element_type=F32)


def dot_nt(a, b):
    return lax.dot_general(a, b, (((1,), (1,)), ((), ())), preferred_element_type=F32)


def dot_tn(a, b):
    return lax.dot_general(a, b, (((0,), (0,)), ((), ())), preferred_element_type=F32)


def center_spread(v):
    c = v - jnp.mean(v, axis=-1, keepdims=True)
    r = lax.rsqrt(jnp.mean(c * c, axis=-1, keepdims=True) + EPS)
    return c, r


def norm(v, gain, shift):
    c, r = center_spread(v)
    return c * r * gain + shift


def norm_back(grad, v, gain):
    c, r = center_spread(v)
    x = c * r
    h = grad * gain
    back = r * (h - jnp.mean(h, axis=-1, keepdims=True) - x * jnp.mean(h * x, axis=-1, keepdims=True))
    return back, colsum(grad * x), colsum(grad)


def colsum(v):
    return jnp.sum(v, axis=0, keepdims=True)


def lane_fold(v):
    total = v[:, :128]
    for k in range(1, v.shape[1] // 128):
        total = total + v[:, k * 128 : (k + 1) * 128]
    return total


def same_bias(seq_row):
    rows = jnp.broadcast_to(seq_row.astype(F32), (ROWS, ROWS))
    return jnp.where(rows == rows.T, 0.0, MASKED)


def aligned(i, size):
    return pl.ds(pl.multiple_of(i * size, size), size)


SAVED = (
    ("src", D, BF16),
    ("qkv", 3 * D, BF16),
    ("mixed", D, BF16),
    ("middle", D, BF16),
    ("xh", FF, BF16),
    ("gp", FF, BF16),
    ("rst", 128, F32),
)
F_OUT = (
    ("normed", D, BF16),
    ("mnormed", D, BF16),
    ("ffn_in", D, BF16),
    ("hn", FF, BF16),
    ("louts", D, BF16),
)
B_OUT = (
    ("dh", FF, BF16),
    ("gml", D, BF16),
    ("gqkv", 3 * D, BF16),
    ("igr", D, BF16),
    ("vec", D, F32),
    ("vecf", FF, F32),
)
STATE = SAVED + F_OUT + B_OUT
SMALL = (("gains", 3, D), ("shifts", 3, D), ("fg", 1, FF), ("fs", 1, FF), ("pb", 4, D), ("ub", 1, FF))
WEIGHTS = (("wqk", D, 2 * D), ("wv", D, D), ("wout", D, D), ("wup", D, FF), ("wdown", FF, D))


def rows_of(name):
    return {"vec": 16, "vecf": 8}.get(name, ROWS)


def inner_forward(v, cp, wait):
    normed_v, qkv, mid, act = v["normed"], v["qkv"], v["mid"], v["act"]
    gains, shifts, fg, fs, pb, ub = (v[n[0]] for n in SMALL)
    u = v["src"][...].astype(F32)
    normed_v[...] = norm(u, gains[0:1], shifts[0:1]).astype(BF16)
    cp.save("normed")
    wait("wqk", "wv")
    cp.load_late("wout", "wup")

    def project(i, _):
        at = aligned(i, 768)
        x = dot_nn(normed_v[...], v["wqkv"][:, at]) + v["qkvb"][0:1, at]
        qkv[:, at] = (x * jnp.where(i == 0, 0.125, 1.0)).astype(BF16)
        return 0

    lax.fori_loop(0, 3, project, 0)
    cp.save_kept("qkv")
    low = lax.broadcasted_iota(jnp.int32, (ROWS, 128), 1) < HEAD_DIM

    def pair(j, _):
        q2 = qkv[:, aligned(j, 128)]
        k2 = qkv[:, aligned(j + PAIRS, 128)]
        v2 = qkv[:, aligned(j + 2 * PAIRS, 128)]
        zero = jnp.zeros_like(k2)
        one = jnp.ones_like(v2)
        sums = []
        for first in (True, False):
            kh = jnp.where(low, k2, zero) if first else jnp.where(low, zero, k2)
            vh = jnp.where(low, v2, one) if first else jnp.where(low, one, v2)
            scores = dot_nt(q2, kh) + v["bias"][...]
            lifted = jnp.exp(scores - jnp.max(scores, axis=-1, keepdims=True)).astype(BF16)
            sums.append(dot_nn(lifted, vh))
        top = jnp.where(low, sums[0], sums[1])
        den = pltpu.roll(jnp.where(low, sums[1], sums[0]), 64, 1)
        mid[:, aligned(j, 128)] = top / den
        return 0

    lax.fori_loop(0, PAIRS, pair, 0, unroll=UNROLL_ATT_F)
    cp.load_late("wdown")
    mixed = mid[...]
    v["mixed"][...] = mixed.astype(BF16)
    cp.save_kept("mixed")
    mnormed = norm(mixed, gains[1:2], shifts[1:2]).astype(BF16)
    v["mnormed"][...] = mnormed
    cp.save("mnormed")
    wait("wout")
    middle = v["src"][...].astype(F32) + dot_nn(mnormed, v["wout"][...]) + pb[2:3]
    mid[...] = middle
    v["middle"][...] = middle.astype(BF16)
    cp.save_kept("middle")
    cp.save_kept("src")
    v["ffn_in"][...] = norm(middle, gains[2:3], shifts[2:3]).astype(BF16)
    cp.save("ffn_in")
    wait("wup")

    def up(i, total):
        at = aligned(i, CH)
        h = dot_nn(v["ffn_in"][...], v["wup"][:, at]) + ub[:, at]
        cdf = 0.5 + 0.5 * lax.erf(h * 0.7071067811865476)
        a = h * cdf
        act[:, at] = a
        pdf = jnp.exp2(h * h * -0.7213475204444817 - 1.3257480647361594)
        v["gp"][:, at] = (cdf + h * pdf).astype(BF16)
        return total + lane_fold(a)

    total = lax.fori_loop(0, N_CH, up, jnp.zeros((ROWS, 128), F32), unroll=UNROLL_UP)
    cp.save_kept("gp")
    mean = jnp.sum(total, axis=-1, keepdims=True) * (1.0 / FF)

    def spread(i, total):
        c = act[:, aligned(i, CH)] - mean
        return total + lane_fold(c * c)

    total = lax.fori_loop(0, N_CH, spread, jnp.zeros((ROWS, 128), F32))
    r = lax.rsqrt(jnp.sum(total, axis=-1, keepdims=True) * (1.0 / FF) + EPS)
    v["rst"][...] = jnp.broadcast_to(r, (ROWS, 128))
    cp.save_kept("rst")
    wait("wdown")
    v["acc"][...] = mid[...] + pb[3:4]

    def down(i, _):
        at = aligned(i, CH)
        x = (act[:, at] - mean) * r
        v["xh"][:, at] = x.astype(BF16)
        hn = (x * fg[:, at] + fs[:, at]).astype(BF16)
        v["hn"][:, at] = hn
        v["acc"][...] += dot_nn(hn, v["wdown"][at, :])
        return 0

    lax.fori_loop(0, N_CH, down, 0, unroll=UNROLL_DOWN)
    v["louts"][...] = v["acc"][...].astype(BF16)
    cp.save("louts")
    cp.save("res")
    cp.save("hn")
    cp.save_kept("xh")


def inner_backward(v, cp, wait, ready):
    gains, fg = v["gains"], v["fg"]
    act, acc, mid, gy_b, xh, gp, qkv, gqkv = (v[n] for n in ("act", "acc", "mid", "gy", "xh", "gp", "qkv", "gqkv"))
    vec, vecf = v["vec"], v["vecf"]
    vec[9:10] = colsum(gy_b[...].astype(F32))
    wait("wdown")
    ready("xh")

    def first(i, totals):
        at = aligned(i, CH)
        g = dot_nt(gy_b[...], v["wdown"][at, :])
        x = xh[:, at].astype(F32)
        gx = g * x
        vecf[0:1, at] = colsum(gx)
        vecf[1:2, at] = colsum(g)
        h = g * fg[:, at]
        act[:, at] = h
        return totals[0] + lane_fold(h), totals[1] + lane_fold(h * x)

    zeros = jnp.zeros((ROWS, 128), F32)
    t1, t2 = lax.fori_loop(0, N_CH, first, (zeros, zeros), unroll=UNROLL_B1)
    m1 = jnp.sum(t1, axis=-1, keepdims=True) * (1.0 / FF)
    m2 = jnp.sum(t2, axis=-1, keepdims=True) * (1.0 / FF)
    ready("gp", "rst")
    wait("wup")
    r = v["rst"][:, 0:1]
    acc[...] = jnp.zeros_like(acc)

    def second(i, _):
        at = aligned(i, CH)
        x = xh[:, at].astype(F32)
        d = (act[:, at] - m1 - x * m2) * r * gp[:, at].astype(F32)
        vecf[2:3, at] = colsum(d)
        low_d = d.astype(BF16)
        v["dh"][:, at] = low_d
        acc[...] += dot_nt(low_d, v["wup"][:, at])
        return 0

    lax.fori_loop(0, N_CH, second, 0, unroll=UNROLL_B2)
    cp.save("dh")
    cp.save("vecf")
    ready("middle")
    back, v_gain, v_shift = norm_back(acc[...], v["middle"][...].astype(F32), gains[2:3])
    vec[2:3] = v_gain
    vec[5:6] = v_shift
    gm = gy_b[...].astype(F32) + back
    mid[...] = gm
    gml_v = gm.astype(BF16)
    v["gml"][...] = gml_v
    cp.save("gml")
    vec[8:9] = colsum(gm)
    wait("wout")
    ready("mixed")
    back, v_gain, v_shift = norm_back(dot_nt(gml_v, v["wout"][...]), v["mixed"][...].astype(F32), gains[1:2])
    vec[1:2] = v_gain
    vec[4:5] = v_shift
    v["gmix"][...] = back.astype(BF16)
    ready("qkv")
    low = lax.broadcasted_iota(jnp.int32, (ROWS, 128), 1) < HEAD_DIM

    def pair(j, _):
        q2 = qkv[:, aligned(j, 128)]
        k2 = qkv[:, aligned(j + PAIRS, 128)]
        v2 = qkv[:, aligned(j + 2 * PAIRS, 128)]
        g2 = v["gmix"][:, aligned(j, 128)]
        zero = jnp.zeros_like(k2)
        gq = gk = gv = None
        for head in range(2):

            def half(t):
                return jnp.where(low, t, zero) if head == 0 else jnp.where(low, zero, t)

            kh, vh, qh, gh = half(k2), half(v2), half(q2), half(g2)
            st = dot_nt(kh, q2) + v["bias"][...]
            e = jnp.exp(st - jnp.max(st, axis=0, keepdims=True))
            p = e * (1.0 / jnp.sum(e, axis=0, keepdims=True))
            gp_t = dot_nt(vh, g2)
            inner = jnp.sum(p * gp_t, axis=0, keepdims=True)
            gs = (p * (gp_t - inner)).astype(BF16)
            a = dot_nn(p.astype(BF16), gh)
            b = dot_nn(gs, qh)
            c = dot_tn(gs, kh * 0.125)
            gv = a if gv is None else gv + a
            gk = b if gk is None else gk + b
            gq = c if gq is None else gq + c
        gqkv[:, aligned(j, 128)] = gq.astype(BF16)
        gqkv[:, aligned(j + PAIRS, 128)] = gk.astype(BF16)
        gqkv[:, aligned(j + 2 * PAIRS, 128)] = gv.astype(BF16)
        vec[6:7, aligned(j, 128)] = colsum(gq)
        vec[7:8, aligned(j, 128)] = colsum(gv)
        return 0

    lax.fori_loop(0, PAIRS, pair, 0, unroll=UNROLL_ATT_B)
    cp.save("gqkv")
    wait("wqk", "wv")
    ready("src")

    def back_chunk(i, _):
        at = aligned(i, 768)
        acc[...] += dot_nt(gqkv[:, at], v["wqkv"][:, at])
        return 0

    acc[...] = jnp.zeros_like(acc)
    lax.fori_loop(0, 3, back_chunk, 0)
    back, v_gain, v_shift = norm_back(acc[...], v["src"][...].astype(F32), gains[0:1])
    vec[0:1] = v_gain
    vec[3:4] = v_shift
    v["igr"][...] = (mid[...] + back).astype(BF16)
    cp.save("send")
    cp.save("igr")
    cp.save("vec")


class Traffic:
    def __init__(self, v, hbm, sems, mb, both):
        self.v, self.hbm, self.sems, self.mb, self.both = v, hbm, sems, mb, both
        self.at = {}
        self.kept = []
        self.late = True

    def sem(self, key):
        return self.sems.at[self.at.setdefault(key, len(self.at))]

    def weight(self, name):
        dst = self.v[name] if name in ("wout", "wup", "wdown") else None
        if name == "wqk":
            dst = self.v["wqkv"].at[:, pl.ds(0, 2 * D)]
        if name == "wv":
            dst = self.v["wqkv"].at[:, pl.ds(2 * D, D)]
        return pltpu.make_async_copy(self.hbm[name].at[0], dst, self.sem(name))

    def load_late(self, *names):
        for n in names:
            self.weight(n).start()

    def out(self, name):
        source = {"res": "louts", "send": "igr"}.get(name, name)
        dst = self.hbm[name] if name in ("res", "send") else self.hbm["o_" + name].at[self.mb]
        return pltpu.make_async_copy(self.v[source], dst, self.sem("o_" + name))

    def save(self, name):
        copy = self.out(name)
        copy.start()
        self.kept.append((name, False))

    def save_kept(self, name):
        copy = self.out(name)
        self.kept.append((name, True))

        @pl.when(jnp.logical_not(self.both))
        def _():
            copy.start()

    def finish(self):
        for name, conditional in self.kept:
            if conditional:

                @pl.when(jnp.logical_not(self.both))
                def _(name=name):
                    self.out(name).wait()
            else:
                self.out(name).wait()
        self.kept = []


def first_of(ref):
    if len(ref.shape) == 3:
        return ref.at[:, 0] if ref.shape[1] == 1 else ref.at[0]
    return ref


def layer_kernel(step, has_f, has_b, n_alias, names_in, *refs):
    n_in = 5 + len(SMALL) + len(WEIGHTS)
    scal, inp_all, f_recv, cot_all, b_recv = refs[:5]
    hbm = dict(zip([n[0] for n in SMALL + WEIGHTS], refs[5:n_in]))
    k = n_in
    ins = dict(zip(names_in, refs[k : k + len(names_in)]))
    seq_h = refs[k + len(names_in)]
    k += len(names_in) + 1 + n_alias
    outs = kernel_outs(has_f, has_b)
    for name in outs:
        hbm["o_" + name if name not in ("res", "send") else name] = refs[k]
        k += 1
    v = dict(zip([n for n, _, _ in kernel_scratch(has_f, has_b)], refs[k:]))
    sems = refs[-1]
    do_f, do_b, mb, sec = scal[3 * step] == 1, scal[3 * step + 1] == 1, scal[3 * step + 2], scal[3 * STEPS]
    only_b = jnp.logical_and(do_b, jnp.logical_not(do_f))

    @pl.when(jnp.logical_or(do_f, do_b))
    def _():
        cp = Traffic(v, hbm, sems, mb, do_b)
        smalls = [pltpu.make_async_copy(first_of(hbm[n]), v[n], cp.sem(n)) for n, _, _ in SMALL]
        seq_copy = pltpu.make_async_copy(seq_h, v["seq"], cp.sem("seq"))
        first_in = pltpu.make_async_copy(first_of(f_recv), v["src"], cp.sem("in")) if has_f else None
        gy_in = pltpu.make_async_copy(first_of(b_recv), v["gy"], cp.sem("gy")) if has_b else None

        def pick(copy, other, own):
            @pl.when(own)
            def _():
                other.start()

            @pl.when(jnp.logical_not(own))
            def _():
                copy.start()

        loads = {n: pltpu.make_async_copy(ins[n].at[mb], v[n], cp.sem("i_" + n)) for n in names_in} if has_b else {}
        if has_f:

            @pl.when(do_f)
            def _():
                pick(first_in, pltpu.make_async_copy(inp_all.at[mb], v["src"], cp.sem("in")), sec == 0)
                cp.load_late("wqk", "wv")

        for c in smalls:
            c.start()
        seq_copy.start()
        if has_b:

            @pl.when(do_b)
            def _():
                pick(gy_in, pltpu.make_async_copy(cot_all.at[mb], v["gy"], cp.sem("gy")), sec != 0)

            @pl.when(only_b)
            def _():
                cp.load_late("wdown")
                for n in ("xh", "gp", "rst"):
                    loads[n].start()
                cp.load_late("wup")
                for n in ("middle", "mixed", "qkv", "src"):
                    loads[n].start()
                cp.load_late("wout", "wqk", "wv")

        seq_copy.wait()
        v["bias"][...] = same_bias(v["seq"][pl.ds(mb, 1), :])
        for c in smalls:
            c.wait()
        if has_f:

            @pl.when(do_f)
            def _():
                v["qkvb"][:, 0:D] = v["pb"][0:1]
                v["qkvb"][:, D : 2 * D] = jnp.zeros((1, D), F32)
                v["qkvb"][:, 2 * D :] = v["pb"][1:2]
                first_in.wait()

                def wait(*names):
                    for n in names:
                        cp.weight(n).wait()

                inner_forward(v, cp, wait)
                if not has_b:
                    cp.finish()

        if has_b:

            @pl.when(do_b)
            def _():
                gy_in.wait()

                def wait(*names):
                    @pl.when(only_b)
                    def _():
                        for n in names:
                            cp.weight(n).wait()

                def ready(*names):
                    @pl.when(only_b)
                    def _():
                        for n in names:
                            loads[n].wait()

                back = Traffic(v, hbm, sems, mb, do_b)
                back.at = cp.at
                inner_backward(v, back, wait, ready)
                back.finish()

            if has_f:

                @pl.when(do_f)
                def _():
                    cp.finish()


def kernel_outs(has_f, has_b):
    names = []
    if has_f:
        names += [n for n, _, _ in SAVED + F_OUT] + ["res"]
    if has_b:
        names += [n for n, _, _ in B_OUT] + ["send"]
    return names


def kernel_scratch(has_f, has_b):
    out = [(n, (r, c), F32) for n, r, c in SMALL]
    out += [("wqkv", (D, 3 * D), BF16)]
    out += [(n, (r, c), BF16) for n, r, c in WEIGHTS[2:]]
    out += [(n, (ROWS, c), t) for n, c, t in SAVED]
    if has_f:
        out += [(n, (ROWS, c), t) for n, c, t in F_OUT] + [("qkvb", (1, 3 * D), F32)]
    if has_b:
        out += [(n, (rows_of(n), c), t) for n, c, t in B_OUT]
        out += [("gy", (ROWS, D), BF16), ("gmix", (ROWS, D), BF16)]
    out += [("seq", (MICRO, ROWS), jnp.int32), ("bias", (ROWS, ROWS), F32)]
    out += [("act", (ROWS, FF), F32), ("acc", (ROWS, D), F32), ("mid", (ROWS, D), F32)]
    return out


def layer_call(step, scal, has_f, has_b, inp, f_recv, cot, b_recv, seq, params, state):
    wqk, wv, wout, wup, wdown, gains, shifts, fg, fs, pb, ub = params
    names_in = tuple(n for n, _, _ in SAVED) if has_b else ()
    outs = kernel_outs(has_f, has_b)
    alias = [n for n in outs if n in state]
    shapes = {n: (rows_of(n), c, t) for n, c, t in STATE}
    out_shape = []
    for n in outs:
        if n in ("res", "send"):
            out_shape.append(jax.ShapeDtypeStruct((ROWS, D), BF16))
        else:
            r, c, t = shapes[n]
            out_shape.append(jax.ShapeDtypeStruct((MICRO, r, c), t))
    separate = () if has_f else names_in
    operands = [scal, inp, f_recv, cot, b_recv, gains, shifts, fg, fs, pb, ub, wqk, wv, wout, wup, wdown]
    operands += [state[n] for n in separate] + [seq]
    base = len(operands)
    operands += [state[n] for n in alias]
    scratch = kernel_scratch(has_f, has_b)

    def body(*refs):
        if has_f and has_b:
            at = base + len(alias)
            by_name = dict(zip(outs, refs[at : at + len(outs)]))
            refs = refs[: base - 1] + tuple(by_name[n] for n in names_in) + refs[base - 1 :]
        layer_kernel(step, has_f, has_b, len(alias), names_in, *refs)

    got = pl.pallas_call(
        body,
        name="layer_" + "f" * has_f + "b" * has_b,
        out_shape=out_shape,
        in_specs=[SM] + [ANY] * (len(operands) - 1),
        out_specs=[ANY] * len(outs),
        scratch_shapes=[pltpu.VMEM(s, t) for _, s, t in scratch] + [pltpu.SemaphoreType.DMA((48,))],
        input_output_aliases={base + i: outs.index(n) for i, n in enumerate(alias)},
        compiler_params=pltpu.CompilerParams(vmem_limit_bytes=VMEM_ALL),
        cost_estimate=LIGHT,
    )(*operands)
    got = dict(zip(outs, got))
    state = dict(state)
    state.update({n: a for n, a in got.items() if n not in ("res", "send")})
    return got.get("res"), got.get("send"), state


TOK = MICRO * ROWS
WIDE = 768
SIDE = 128
ORDER = ("down", "up0", "up1", "att0", "att1", "down", "up0", "up1", "up0", "att0", "up1", "att1", "att0", "att1")


def grad_down_kernel(scal, hn, cot, q0, q1, q2, send, keep, hn_v, gy, out, sems):
    core = scal[0]
    half, rows = send.shape[0], send.shape[1]
    per = half * 2 * rows // (FF // WIDE) // (2 * rows)
    own = [pltpu.make_async_copy(q, gy.at[pl.ds(i * ROWS, ROWS)], sems.at[i]) for i, q in enumerate((q0, q1, q2))]
    given = pltpu.make_async_copy(cot, gy, sems.at[0])

    def load(g):
        at = aligned(g, WIDE)
        return pltpu.make_async_copy(hn.at[:, at], hn_v.at[:, at], sems.at[4 + g])

    def store(g):
        at = pl.ds(g * per, per)
        return (
            pltpu.make_async_copy(out.at[0, at], send.at[at], sems.at[8 + g]),
            pltpu.make_async_copy(out.at[1, at], keep.at[at], sems.at[12 + g]),
        )

    @pl.when(scal[1] == 0)
    def _():
        for c in own:
            c.start()

    @pl.when(scal[1] != 0)
    def _():
        given.start()

    for g in range(FF // WIDE):
        load(g).start()

    @pl.when(scal[1] == 0)
    def _():
        for c in own:
            c.wait()

    @pl.when(scal[1] != 0)
    def _():
        given.wait()

    def group(g, _):
        load(g).wait()
        for k in range(per):
            j = g * per + k
            r = dot_tn(hn_v[:, aligned(j, 2 * rows)], gy[...])
            out[1 - core, j] = r[:rows].astype(BF16)
            out[core, j] = r[rows:].astype(BF16)
        for c in store(g):
            c.start()
        return 0

    lax.fori_loop(0, FF // WIDE, group, 0)
    for g in range(FF // WIDE):
        for c in store(g):
            c.wait()


def down_call(scal, hn, cot, qs, n_dp):
    rows = FF // n_dp
    half = n_dp // 2
    shape = jax.ShapeDtypeStruct((half, rows, D), BF16)
    return pl.pallas_call(
        grad_down_kernel,
        name="grad_down",
        out_shape=[shape, shape],
        in_specs=[SM] + [ANY] * 5,
        out_specs=[ANY] * 2,
        scratch_shapes=[
            pltpu.VMEM((TOK, FF), BF16),
            pltpu.VMEM((TOK, D), BF16),
            pltpu.VMEM((2, half, rows, D), BF16),
            pltpu.SemaphoreType.DMA((16,)),
        ],
        compiler_params=pltpu.CompilerParams(vmem_limit_bytes=VMEM_ALL),
        cost_estimate=LIGHT,
    )(scal, hn.reshape(TOK, FF), cot.reshape(TOK, D), *qs)


def wide_kernel(n_left, n_right, parts, extra, *refs):
    n_in = 1 + n_left + n_right + extra
    scal, lefts, rights = refs[0], refs[1 : 1 + n_left], refs[1 + n_left : 1 + n_left + n_right]
    dsts = refs[n_in:][: 2 * parts]
    left_v, right_v, turned, out, sems = refs[n_in + 2 * parts :][:5]
    core = scal[0]
    half, rows = out.shape[1], out.shape[2]
    groups = right_v.shape[1] // WIDE
    per = groups // parts
    sources = [(r, k) for r in rights for k in range(r.shape[1] // WIDE)]
    left_copies = [pltpu.make_async_copy(x, left_v.at[i], sems.at[i]) for i, x in enumerate(lefts)]
    for c in left_copies:
        c.start()
    loads = []
    for g, (r, k) in enumerate(sources):
        c = pltpu.make_async_copy(r.at[:, pl.ds(k * WIDE, WIDE)], right_v.at[:, pl.ds(g * WIDE, WIDE)], sems.at[2 + g])
        c.start()
        loads.append(c)
    if extra:
        side_v = refs[-1]
        side_copy = pltpu.make_async_copy(refs[n_in - 1], side_v, sems.at[15])
        side_copy.start()
    for i, c in enumerate(left_copies):
        c.wait()
        turned[i] = left_v[i].T

    def put(r, at):
        for j in range(half):
            out[1 - core, j, :, at] = r[2 * j * rows : (2 * j + 1) * rows].astype(BF16)
            out[core, j, :, at] = r[(2 * j + 1) * rows : (2 * j + 2) * rows].astype(BF16)

    def product(g, _):
        at = aligned(g, WIDE)
        which = 0 if n_left == 1 else jnp.where(g >= groups - 1, 1, 0)
        put(dot_nn(turned[which], right_v[:, at]), at)
        return 0

    if extra:
        side_copy.wait()
        put(side_v[...], pl.ds(groups * WIDE, SIDE))
    stores = []
    for p in range(parts):
        for g in range(p * per, (p + 1) * per):
            loads[g].wait()
        lax.fori_loop(p * per, (p + 1) * per, product, 0)
        width = dsts[2 * p].shape[2]
        for side in range(2):
            c = pltpu.make_async_copy(
                out.at[side, :, :, pl.ds(p * per * WIDE, width)], dsts[2 * p + side], sems.at[6 + 2 * p + side]
            )
            c.start()
            stores.append(c)
    for c in stores:
        c.wait()


def wide_call(name, scal, lefts, rights, parts, n_dp, extra=None):
    rows = D // n_dp
    half = n_dp // 2
    cols = sum(r.shape[1] for r in rights)
    widths = [cols // parts] * parts
    if extra is not None:
        widths[-1] += SIDE
    shapes = [jax.ShapeDtypeStruct((half, rows, w), BF16) for w in widths for _ in range(2)]
    more = [] if extra is None else [extra]
    return pl.pallas_call(
        functools.partial(wide_kernel, len(lefts), len(rights), parts, len(more)),
        name=name,
        out_shape=shapes,
        in_specs=[SM] + [ANY] * (len(lefts) + len(rights) + len(more)),
        out_specs=[ANY] * (2 * parts),
        scratch_shapes=[
            pltpu.VMEM((len(lefts), TOK, D), BF16),
            pltpu.VMEM((TOK, cols), BF16),
            pltpu.VMEM((len(lefts), D, TOK), BF16),
            pltpu.VMEM((2, half, rows, sum(widths)), BF16),
            pltpu.SemaphoreType.DMA((16,)),
        ]
        + [pltpu.VMEM((D, SIDE), F32)] * len(more),
        compiler_params=pltpu.CompilerParams(vmem_limit_bytes=VMEM_ALL),
        cost_estimate=LIGHT,
    )(scal, *lefts, *rights, *more)


def merge_kernel(mine, ka, ga, kb, gb, send, keep):
    send[...] = (ka[...].astype(F32) + ga[...].astype(F32)).astype(BF16)
    keep[...] = (kb[...].astype(F32) + gb[...].astype(F32)).astype(BF16)


def merge(keep, got, mine):
    count, rows, cols = keep.shape
    shape = jax.ShapeDtypeStruct((count // 2, rows, cols), BF16)
    other = pl.BlockSpec((None, None, rows, cols), lambda i, m: (i, 1 - m[0], 0, 0))
    own = pl.BlockSpec((None, None, rows, cols), lambda i, m: (i, m[0], 0, 0))
    out = pl.BlockSpec((None, rows, cols), lambda i, m: (i, 0, 0))
    keep, got = (t.reshape(count // 2, 2, rows, cols) for t in (keep, got))
    return pl.pallas_call(
        merge_kernel,
        name="merge_halves",
        grid_spec=pltpu.PrefetchScalarGridSpec(
            num_scalar_prefetch=1, grid=(count // 2,), in_specs=[other, other, own, own], out_specs=[out, out]
        ),
        out_shape=[shape, shape],
        compiler_params=pltpu.CompilerParams(vmem_limit_bytes=VMEM_ALL),
        cost_estimate=LIGHT,
    )(mine, keep, got, keep, got)


def swap(x, bit, n_dp):
    return lax.ppermute(x, "dp", [(i, i ^ bit) for i in range(n_dp)])


def after(x, *others):
    return lax.optimization_barrier((x,) + others)[0]


class Exchange:
    def __init__(self, n_dp):
        self.n_dp = n_dp
        self.me = lax.axis_index("dp")
        self.last = None

    def step(self, chunk):
        send, keep, bit = chunk
        mine = (self.me // (2 * bit) % 2).astype(jnp.int32)[None]
        if self.last is not None:
            mine = after(mine, *self.last)
        self.last = merge(keep, swap(send, bit, self.n_dp), mine)
        return (*self.last, 2 * bit)

    def finish(self, chunk):
        send, keep, bit = chunk
        got = swap(send, bit, self.n_dp)
        return keep[0].astype(F32) + got[0].astype(F32)


def token_product(left, right):
    left, right = (t.reshape(TOK, t.shape[-1]) for t in (left, right))
    return lax.psum_scatter(dot_tn(left, right), "dp", scatter_dimension=0, tiled=True)


def token_sum(rows):
    return lax.psum_scatter(rows, "dp", scatter_dimension=1, tiled=True)


def shifted(x, by):
    length = lax.axis_size("section")
    pairs = [(i, i + by) for i in range(length) if 0 <= i + by < length]
    return lax.ppermute(x, "section", pairs)


def local(n_dp, inputs, out_cotangent, sequence_ids, *raw):
    params = raw[:5] + tuple(jnp.transpose(t, (1, 0, 2)) for t in raw[5:7]) + raw[7:]
    sec = lax.axis_index("section")
    me = lax.axis_index("dp")
    inp = inputs.reshape(MICRO, ROWS, D)
    cot = out_cotangent.reshape(MICRO, ROWS, D)
    seq = sequence_ids

    def code(f, b):
        mb = next((m for m in (f, b) if m is not None), 0)
        return [int(f is not None), int(b is not None), mb]

    plan = [(0, None, None, None), (1, None, None, None), (2, None, 0, 0), (None, None, 1, 1)]
    plan += [(None, 0, 2, 2), (None, 1, None, None), (None, 2, None, None)]
    first = [x for f0, b0, _, _ in plan for x in code(f0, b0)] + [0]
    second = [x for _, _, f1, b1 in plan for x in code(f1, b1)] + [1]
    table = jnp.where(sec == 0, jnp.array(first, jnp.int32), jnp.array(second, jnp.int32))
    none = inp
    state = {}

    def run(step, f_recv=none, b_recv=none, wait_for=()):
        nonlocal state
        f0, b0, f1, b1 = plan[step]
        has_f, has_b = f0 is not None or f1 is not None, b0 is not None or b1 is not None
        scal = after(table, *wait_for) if wait_for else table
        res, send, state = layer_call(step, scal, has_f, has_b, inp, f_recv, cot, b_recv, seq, params, state)
        return res, send

    r0, _ = run(0)
    p0 = shifted(r0, 1)
    r1, _ = run(1)
    p1 = shifted(r1, 1)
    r2, g0 = run(2, f_recv=p0)
    p2 = shifted(r2, 1)
    q0 = shifted(g0, -1)
    _, g1 = run(3, f_recv=p1)
    q1 = shifted(g1, -1)
    _, g2 = run(4, f_recv=p2, b_recv=q0)
    q2 = shifted(g2, -1)
    run(5, b_recv=q1)
    core = jnp.stack([me % 2, sec]).astype(jnp.int32)
    blocks = n_dp == 16
    done = ()
    if blocks:
        ex = Exchange(n_dp)
        down = ex.step((*down_call(after(core, state["gml"]), state["hn"], cot, (q0, q1, q2), n_dp), 1))
        done = ex.last
    run(6, b_recv=q2, wait_for=done)
    vec = jnp.sum(state["vec"], axis=0)
    vecf = jnp.sum(state["vecf"], axis=0)
    n1, n2 = D // n_dp, FF // n_dp
    if blocks:
        flat = {n: state[n].reshape(TOK, state[n].shape[-1]) for n in ("ffn_in", "dh", "normed", "mnormed", "gqkv", "gml")}
        side = [vec[:10].T, vecf[:3].reshape(3, n_dp, n2 // n1, n1).transpose(1, 3, 0, 2).reshape(D, -1)]
        used = 10 + 3 * (n2 // n1)
        side = jnp.concatenate(side + [jnp.zeros((D, SIDE - used), F32)], axis=1)
        att = wide_call("grad_attn", core, (flat["normed"], flat["mnormed"]), (flat["gqkv"], flat["gml"]), 2, n_dp)
        up = wide_call("grad_up", after(core, att[0]), (flat["ffn_in"],), (flat["dh"],), 2, n_dp, side)
        chunk = {"down": down}
        chunk.update({n: (*t, 1) for n, t in (("up0", up[:2]), ("up1", up[2:]), ("att0", att[:2]), ("att1", att[2:]))})
        ex.last = ex.last + up[:1]
        for n in ORDER:
            chunk[n] = ex.step(chunk[n])
        g_down, g_up0, g_up1, g_qk, g_vo = (ex.finish(chunk[n]) for n in ("down", "up0", "up1", "att0", "att1"))
        g_up = jnp.concatenate([g_up0, g_up1[:, : FF // 2]], axis=1)
        g_att = jnp.concatenate([g_qk, g_vo], axis=1)
        g_side = g_up1[:, FF // 2 : FF // 2 + used]
        va = g_side[:, :10].T
        vb = g_side[:, 10:].reshape(n1, 3, n2 // n1).transpose(1, 2, 0).reshape(3, n2)
    else:
        gy = jnp.where(sec == 0, jnp.stack([q0, q1, q2]), cot)
        g_down = token_product(state["hn"], gy)
        g_up = token_product(state["ffn_in"], state["dh"])
        g_att = jnp.concatenate(
            [token_product(state["normed"], state["gqkv"]), token_product(state["mnormed"], state["gml"])], axis=1
        )
        va = token_sum(vec[:10])
        vb = token_sum(vecf[:3])
    rows = MICRO * ROWS
    return (
        state["louts"].reshape(1, rows, D),
        state["igr"].reshape(1, rows, D),
        g_att[None, :, : 2 * D],
        g_att[None, :, 2 * D : 3 * D],
        g_att[None, :, 3 * D :],
        g_up[None],
        g_down[None],
        va[0:3][None],
        va[3:6][None],
        vb[0:1],
        vb[1:2],
        va[6:10][None],
        vb[2:3],
    )


def solution(mesh):
    in_specs = (
        P("dp", None),
        P("dp", None),
        P("dp", None),
        P("section", None, None),
        P("section", None, None),
        P("section", None, None),
        P("section", None, None),
        P("section", None, None),
        P("section", None, None),
        P("section", None, None),
        P("section", None),
        P("section", None),
        P("section", None, None),
        P("section", None),
    )
    out_specs = (
        P("section", "dp", None),
        P("section", "dp", None),
        P("section", "dp", None),
        P("section", "dp", None),
        P("section", "dp", None),
        P("section", "dp", None),
        P("section", "dp", None),
        P("section", None, "dp"),
        P("section", None, "dp"),
        P("section", "dp"),
        P("section", "dp"),
        P("section", None, "dp"),
        P("section", "dp"),
    )
    body = functools.partial(local, mesh.shape["dp"])
    return jax.shard_map(body, mesh=mesh, in_specs=in_specs, out_specs=out_specs, check_vma=False)
```

```python
import functools

import jax
import jax.numpy as jnp
from jax import lax
from jax.experimental import pallas as pl
from jax.experimental.pallas import tpu as pltpu
from jax.sharding import PartitionSpec as P

D = 768
HEADS = 12
HEAD_DIM = 64
FF = 3072
ROWS = 256
MICRO = 3
EPS = 1e-05
MASKED = -1e30
CH = 768
N_CH = FF // CH
UNROLL_ATT_F = 6
UNROLL_ATT_B = 2
UNROLL_UP = 2
UNROLL_DOWN = 2
UNROLL_B1 = 2
UNROLL_B2 = 2
VMEM_ALL = 63 << 20
LIGHT = pl.CostEstimate(flops=1000, bytes_accessed=1000, transcendentals=0)
STEPS = 7
HEAVY = pl.CostEstimate(flops=2 * 10**10, bytes_accessed=10 << 20, transcendentals=0)
PAIRS = HEADS // 2
F32 = jnp.float32
BF16 = jnp.bfloat16
ANY = pl.BlockSpec(memory_space=pl.ANY)
VM = pl.BlockSpec(memory_space=pltpu.VMEM)
SM = pl.BlockSpec(memory_space=pltpu.SMEM)


def dot_nn(a, b):
    return lax.dot_general(a, b, (((1,), (0,)), ((), ())), preferred_element_type=F32)


def dot_nt(a, b):
    return lax.dot_general(a, b, (((1,), (1,)), ((), ())), preferred_element_type=F32)


def dot_tn(a, b):
    return lax.dot_general(a, b, (((0,), (0,)), ((), ())), preferred_element_type=F32)


def center_spread(v):
    c = v - jnp.mean(v, axis=-1, keepdims=True)
    r = lax.rsqrt(jnp.mean(c * c, axis=-1, keepdims=True) + EPS)
    return c, r


def norm(v, gain, shift):
    c, r = center_spread(v)
    return c * r * gain + shift


def norm_back(grad, v, gain):
    c, r = center_spread(v)
    x = c * r
    h = grad * gain
    back = r * (h - jnp.mean(h, axis=-1, keepdims=True) - x * jnp.mean(h * x, axis=-1, keepdims=True))
    return back, colsum(grad * x), colsum(grad)


def colsum(v):
    return jnp.sum(v, axis=0, keepdims=True)


def lane_fold(v):
    total = v[:, :128]
    for k in range(1, v.shape[1] // 128):
        total = total + v[:, k * 128 : (k + 1) * 128]
    return total


def same_bias(seq_row):
    rows = jnp.broadcast_to(seq_row.astype(F32), (ROWS, ROWS))
    return jnp.where(rows == rows.T, 0.0, MASKED)


def aligned(i, size):
    return pl.ds(pl.multiple_of(i * size, size), size)


SAVED = (
    ("src", D, BF16),
    ("qkv", 3 * D, BF16),
    ("mixed", D, BF16),
    ("middle", D, BF16),
    ("xh", FF, BF16),
    ("gp", FF, BF16),
    ("rst", 128, F32),
)
F_OUT = (
    ("normed", D, BF16),
    ("mnormed", D, BF16),
    ("ffn_in", D, BF16),
    ("hn", FF, BF16),
    ("louts", D, BF16),
)
B_OUT = (
    ("dh", FF, BF16),
    ("gml", D, BF16),
    ("gqkv", 3 * D, BF16),
    ("igr", D, BF16),
    ("vec", D, F32),
    ("vecf", FF, F32),
)
STATE = SAVED + F_OUT + B_OUT
SMALL = (("gains", 3, D), ("shifts", 3, D), ("fg", 1, FF), ("fs", 1, FF), ("pb", 4, D), ("ub", 1, FF))
WEIGHTS = (("wqk", D, 2 * D), ("wv", D, D), ("wout", D, D), ("wup", D, FF), ("wdown", FF, D))


def rows_of(name):
    return {"vec": 16, "vecf": 8}.get(name, ROWS)


def inner_forward(v, cp, wait):
    normed_v, qkv, mid, act = v["normed"], v["qkv"], v["mid"], v["act"]
    gains, shifts, fg, fs, pb, ub = (v[n[0]] for n in SMALL)
    u = v["src"][...].astype(F32)
    normed_v[...] = norm(u, gains[0:1], shifts[0:1]).astype(BF16)
    cp.save("normed")
    wait("wqk", "wv")
    cp.load_late("wout", "wup")

    def project(i, _):
        at = aligned(i, 768)
        x = dot_nn(normed_v[...], v["wqkv"][:, at]) + v["qkvb"][0:1, at]
        qkv[:, at] = (x * jnp.where(i == 0, 0.125, 1.0)).astype(BF16)
        return 0

    lax.fori_loop(0, 3, project, 0)
    cp.save_kept("qkv")
    low = lax.broadcasted_iota(jnp.int32, (ROWS, 128), 1) < HEAD_DIM

    def pair(j, _):
        q2 = qkv[:, aligned(j, 128)]
        k2 = qkv[:, aligned(j + PAIRS, 128)]
        v2 = qkv[:, aligned(j + 2 * PAIRS, 128)]
        zero = jnp.zeros_like(k2)
        one = jnp.ones_like(v2)
        sums = []
        for first in (True, False):
            kh = jnp.where(low, k2, zero) if first else jnp.where(low, zero, k2)
            vh = jnp.where(low, v2, one) if first else jnp.where(low, one, v2)
            scores = dot_nt(q2, kh) + v["bias"][...]
            lifted = jnp.exp(scores - jnp.max(scores, axis=-1, keepdims=True)).astype(BF16)
            sums.append(dot_nn(lifted, vh))
        top = jnp.where(low, sums[0], sums[1])
        den = pltpu.roll(jnp.where(low, sums[1], sums[0]), 64, 1)
        mid[:, aligned(j, 128)] = top / den
        return 0

    lax.fori_loop(0, PAIRS, pair, 0, unroll=UNROLL_ATT_F)
    cp.load_late("wdown")
    mixed = mid[...]
    v["mixed"][...] = mixed.astype(BF16)
    cp.save_kept("mixed")
    mnormed = norm(mixed, gains[1:2], shifts[1:2]).astype(BF16)
    v["mnormed"][...] = mnormed
    cp.save("mnormed")
    wait("wout")
    middle = v["src"][...].astype(F32) + dot_nn(mnormed, v["wout"][...]) + pb[2:3]
    mid[...] = middle
    v["middle"][...] = middle.astype(BF16)
    cp.save_kept("middle")
    cp.save_kept("src")
    v["ffn_in"][...] = norm(middle, gains[2:3], shifts[2:3]).astype(BF16)
    cp.save("ffn_in")
    wait("wup")

    def up(i, total):
        at = aligned(i, CH)
        h = dot_nn(v["ffn_in"][...], v["wup"][:, at]) + ub[:, at]
        cdf = 0.5 + 0.5 * lax.erf(h * 0.7071067811865476)
        a = h * cdf
        act[:, at] = a
        pdf = jnp.exp2(h * h * -0.7213475204444817 - 1.3257480647361594)
        v["gp"][:, at] = (cdf + h * pdf).astype(BF16)
        return total + lane_fold(a)

    total = lax.fori_loop(0, N_CH, up, jnp.zeros((ROWS, 128), F32), unroll=UNROLL_UP)
    cp.save_kept("gp")
    mean = jnp.sum(total, axis=-1, keepdims=True) * (1.0 / FF)

    def spread(i, total):
        c = act[:, aligned(i, CH)] - mean
        return total + lane_fold(c * c)

    total = lax.fori_loop(0, N_CH, spread, jnp.zeros((ROWS, 128), F32))
    r = lax.rsqrt(jnp.sum(total, axis=-1, keepdims=True) * (1.0 / FF) + EPS)
    v["rst"][...] = jnp.broadcast_to(r, (ROWS, 128))
    cp.save_kept("rst")
    wait("wdown")
    v["acc"][...] = mid[...] + pb[3:4]

    def down(i, _):
        at = aligned(i, CH)
        x = (act[:, at] - mean) * r
        v["xh"][:, at] = x.astype(BF16)
        hn = (x * fg[:, at] + fs[:, at]).astype(BF16)
        v["hn"][:, at] = hn
        v["acc"][...] += dot_nn(hn, v["wdown"][at, :])
        return 0

    lax.fori_loop(0, N_CH, down, 0, unroll=UNROLL_DOWN)
    v["louts"][...] = v["acc"][...].astype(BF16)
    cp.save("louts")
    cp.save("res")
    cp.save("hn")
    cp.save_kept("xh")


def inner_backward(v, cp, wait, ready):
    gains, fg = v["gains"], v["fg"]
    act, acc, mid, gy_b, xh, gp, qkv, gqkv = (v[n] for n in ("act", "acc", "mid", "gy", "xh", "gp", "qkv", "gqkv"))
    vec, vecf = v["vec"], v["vecf"]
    vec[9:10] = colsum(gy_b[...].astype(F32))
    wait("wdown")
    ready("xh")

    def first(i, totals):
        at = aligned(i, CH)
        g = dot_nt(gy_b[...], v["wdown"][at, :])
        x = xh[:, at].astype(F32)
        gx = g * x
        vecf[0:1, at] = colsum(gx)
        vecf[1:2, at] = colsum(g)
        h = g * fg[:, at]
        act[:, at] = h
        return totals[0] + lane_fold(h), totals[1] + lane_fold(h * x)

    zeros = jnp.zeros((ROWS, 128), F32)
    t1, t2 = lax.fori_loop(0, N_CH, first, (zeros, zeros), unroll=UNROLL_B1)
    m1 = jnp.sum(t1, axis=-1, keepdims=True) * (1.0 / FF)
    m2 = jnp.sum(t2, axis=-1, keepdims=True) * (1.0 / FF)
    ready("gp", "rst")
    wait("wup")
    r = v["rst"][:, 0:1]
    acc[...] = jnp.zeros_like(acc)

    def second(i, _):
        at = aligned(i, CH)
        x = xh[:, at].astype(F32)
        d = (act[:, at] - m1 - x * m2) * r * gp[:, at].astype(F32)
        vecf[2:3, at] = colsum(d)
        low_d = d.astype(BF16)
        v["dh"][:, at] = low_d
        acc[...] += dot_nt(low_d, v["wup"][:, at])
        return 0

    lax.fori_loop(0, N_CH, second, 0, unroll=UNROLL_B2)
    cp.save("dh")
    cp.save("vecf")
    ready("middle")
    back, v_gain, v_shift = norm_back(acc[...], v["middle"][...].astype(F32), gains[2:3])
    vec[2:3] = v_gain
    vec[5:6] = v_shift
    gm = gy_b[...].astype(F32) + back
    mid[...] = gm
    gml_v = gm.astype(BF16)
    v["gml"][...] = gml_v
    cp.save("gml")
    vec[8:9] = colsum(gm)
    wait("wout")
    ready("mixed")
    back, v_gain, v_shift = norm_back(dot_nt(gml_v, v["wout"][...]), v["mixed"][...].astype(F32), gains[1:2])
    vec[1:2] = v_gain
    vec[4:5] = v_shift
    v["gmix"][...] = back.astype(BF16)
    ready("qkv")
    low = lax.broadcasted_iota(jnp.int32, (ROWS, 128), 1) < HEAD_DIM

    def pair(j, _):
        q2 = qkv[:, aligned(j, 128)]
        k2 = qkv[:, aligned(j + PAIRS, 128)]
        v2 = qkv[:, aligned(j + 2 * PAIRS, 128)]
        g2 = v["gmix"][:, aligned(j, 128)]
        zero = jnp.zeros_like(k2)
        gq = gk = gv = None
        for head in range(2):

            def half(t):
                return jnp.where(low, t, zero) if head == 0 else jnp.where(low, zero, t)

            kh, vh, qh, gh = half(k2), half(v2), half(q2), half(g2)
            st = dot_nt(kh, q2) + v["bias"][...]
            e = jnp.exp(st - jnp.max(st, axis=0, keepdims=True))
            p = e * (1.0 / jnp.sum(e, axis=0, keepdims=True))
            gp_t = dot_nt(vh, g2)
            inner = jnp.sum(p * gp_t, axis=0, keepdims=True)
            gs = (p * (gp_t - inner)).astype(BF16)
            a = dot_nn(p.astype(BF16), gh)
            b = dot_nn(gs, qh)
            c = dot_tn(gs, kh * 0.125)
            gv = a if gv is None else gv + a
            gk = b if gk is None else gk + b
            gq = c if gq is None else gq + c
        gqkv[:, aligned(j, 128)] = gq.astype(BF16)
        gqkv[:, aligned(j + PAIRS, 128)] = gk.astype(BF16)
        gqkv[:, aligned(j + 2 * PAIRS, 128)] = gv.astype(BF16)
        vec[6:7, aligned(j, 128)] = colsum(gq)
        vec[7:8, aligned(j, 128)] = colsum(gv)
        return 0

    lax.fori_loop(0, PAIRS, pair, 0, unroll=UNROLL_ATT_B)
    cp.save("gqkv")
    wait("wqk", "wv")
    ready("src")

    def back_chunk(i, _):
        at = aligned(i, 768)
        acc[...] += dot_nt(gqkv[:, at], v["wqkv"][:, at])
        return 0

    acc[...] = jnp.zeros_like(acc)
    lax.fori_loop(0, 3, back_chunk, 0)
    back, v_gain, v_shift = norm_back(acc[...], v["src"][...].astype(F32), gains[0:1])
    vec[0:1] = v_gain
    vec[3:4] = v_shift
    v["igr"][...] = (mid[...] + back).astype(BF16)
    cp.save("send")
    cp.save("igr")
    cp.save("vec")


class Traffic:
    def __init__(self, v, hbm, sems, mb, both):
        self.v, self.hbm, self.sems, self.mb, self.both = v, hbm, sems, mb, both
        self.at = {}
        self.kept = []
        self.late = True

    def sem(self, key):
        return self.sems.at[self.at.setdefault(key, len(self.at))]

    def weight(self, name):
        dst = self.v[name] if name in ("wout", "wup", "wdown") else None
        if name == "wqk":
            dst = self.v["wqkv"].at[:, pl.ds(0, 2 * D)]
        if name == "wv":
            dst = self.v["wqkv"].at[:, pl.ds(2 * D, D)]
        return pltpu.make_async_copy(self.hbm[name].at[0], dst, self.sem(name))

    def load_late(self, *names):
        for n in names:
            self.weight(n).start()

    def out(self, name):
        source = {"res": "louts", "send": "igr"}.get(name, name)
        dst = self.hbm[name] if name in ("res", "send") else self.hbm["o_" + name].at[self.mb]
        return pltpu.make_async_copy(self.v[source], dst, self.sem("o_" + name))

    def save(self, name):
        copy = self.out(name)
        copy.start()
        self.kept.append((name, False))

    def save_kept(self, name):
        copy = self.out(name)
        self.kept.append((name, True))

        @pl.when(jnp.logical_not(self.both))
        def _():
            copy.start()

    def finish(self):
        for name, conditional in self.kept:
            if conditional:

                @pl.when(jnp.logical_not(self.both))
                def _(name=name):
                    self.out(name).wait()
            else:
                self.out(name).wait()
        self.kept = []


def first_of(ref):
    if len(ref.shape) == 3:
        return ref.at[:, 0] if ref.shape[1] == 1 else ref.at[0]
    return ref


def layer_kernel(step, has_f, has_b, n_alias, names_in, *refs):
    n_in = 5 + len(SMALL) + len(WEIGHTS)
    scal, inp_all, f_recv, cot_all, b_recv = refs[:5]
    hbm = dict(zip([n[0] for n in SMALL + WEIGHTS], refs[5:n_in]))
    k = n_in
    ins = dict(zip(names_in, refs[k : k + len(names_in)]))
    seq_h = refs[k + len(names_in)]
    k += len(names_in) + 1 + n_alias
    outs = kernel_outs(has_f, has_b)
    for name in outs:
        hbm["o_" + name if name not in ("res", "send") else name] = refs[k]
        k += 1
    v = dict(zip([n for n, _, _ in kernel_scratch(has_f, has_b)], refs[k:]))
    sems = refs[-1]
    do_f, do_b, mb, sec = scal[3 * step] == 1, scal[3 * step + 1] == 1, scal[3 * step + 2], scal[3 * STEPS]
    only_b = jnp.logical_and(do_b, jnp.logical_not(do_f))

    @pl.when(jnp.logical_or(do_f, do_b))
    def _():
        cp = Traffic(v, hbm, sems, mb, do_b)
        smalls = [pltpu.make_async_copy(first_of(hbm[n]), v[n], cp.sem(n)) for n, _, _ in SMALL]
        seq_copy = pltpu.make_async_copy(seq_h, v["seq"], cp.sem("seq"))
        first_in = pltpu.make_async_copy(first_of(f_recv), v["src"], cp.sem("in")) if has_f else None
        gy_in = pltpu.make_async_copy(first_of(b_recv), v["gy"], cp.sem("gy")) if has_b else None

        def pick(copy, other, own):
            @pl.when(own)
            def _():
                other.start()

            @pl.when(jnp.logical_not(own))
            def _():
                copy.start()

        loads = {n: pltpu.make_async_copy(ins[n].at[mb], v[n], cp.sem("i_" + n)) for n in names_in} if has_b else {}
        if has_f:

            @pl.when(do_f)
            def _():
                pick(first_in, pltpu.make_async_copy(inp_all.at[mb], v["src"], cp.sem("in")), sec == 0)
                cp.load_late("wqk", "wv")

        for c in smalls:
            c.start()
        seq_copy.start()
        if has_b:

            @pl.when(do_b)
            def _():
                pick(gy_in, pltpu.make_async_copy(cot_all.at[mb], v["gy"], cp.sem("gy")), sec != 0)

            @pl.when(only_b)
            def _():
                cp.load_late("wdown")
                for n in ("xh", "gp", "rst"):
                    loads[n].start()
                cp.load_late("wup")
                for n in ("middle", "mixed", "qkv", "src"):
                    loads[n].start()
                cp.load_late("wout", "wqk", "wv")

        seq_copy.wait()
        v["bias"][...] = same_bias(v["seq"][pl.ds(mb, 1), :])
        for c in smalls:
            c.wait()
        if has_f:

            @pl.when(do_f)
            def _():
                v["qkvb"][:, 0:D] = v["pb"][0:1]
                v["qkvb"][:, D : 2 * D] = jnp.zeros((1, D), F32)
                v["qkvb"][:, 2 * D :] = v["pb"][1:2]
                first_in.wait()

                def wait(*names):
                    for n in names:
                        cp.weight(n).wait()

                inner_forward(v, cp, wait)
                if not has_b:
                    cp.finish()

        if has_b:

            @pl.when(do_b)
            def _():
                gy_in.wait()

                def wait(*names):
                    @pl.when(only_b)
                    def _():
                        for n in names:
                            cp.weight(n).wait()

                def ready(*names):
                    @pl.when(only_b)
                    def _():
                        for n in names:
                            loads[n].wait()

                back = Traffic(v, hbm, sems, mb, do_b)
                back.at = cp.at
                inner_backward(v, back, wait, ready)
                back.finish()

            if has_f:

                @pl.when(do_f)
                def _():
                    cp.finish()


def kernel_outs(has_f, has_b):
    names = []
    if has_f:
        names += [n for n, _, _ in SAVED + F_OUT] + ["res"]
    if has_b:
        names += [n for n, _, _ in B_OUT] + ["send"]
    return names


def kernel_scratch(has_f, has_b):
    out = [(n, (r, c), F32) for n, r, c in SMALL]
    out += [("wqkv", (D, 3 * D), BF16)]
    out += [(n, (r, c), BF16) for n, r, c in WEIGHTS[2:]]
    out += [(n, (ROWS, c), t) for n, c, t in SAVED]
    if has_f:
        out += [(n, (ROWS, c), t) for n, c, t in F_OUT] + [("qkvb", (1, 3 * D), F32)]
    if has_b:
        out += [(n, (rows_of(n), c), t) for n, c, t in B_OUT]
        out += [("gy", (ROWS, D), BF16), ("gmix", (ROWS, D), BF16)]
    out += [("seq", (MICRO, ROWS), jnp.int32), ("bias", (ROWS, ROWS), F32)]
    out += [("act", (ROWS, FF), F32), ("acc", (ROWS, D), F32), ("mid", (ROWS, D), F32)]
    return out


def layer_call(step, scal, has_f, has_b, inp, f_recv, cot, b_recv, seq, params, state):
    wqk, wv, wout, wup, wdown, gains, shifts, fg, fs, pb, ub = params
    names_in = tuple(n for n, _, _ in SAVED) if has_b else ()
    outs = kernel_outs(has_f, has_b)
    alias = [n for n in outs if n in state]
    shapes = {n: (rows_of(n), c, t) for n, c, t in STATE}
    out_shape = []
    for n in outs:
        if n in ("res", "send"):
            out_shape.append(jax.ShapeDtypeStruct((ROWS, D), BF16))
        else:
            r, c, t = shapes[n]
            out_shape.append(jax.ShapeDtypeStruct((MICRO, r, c), t))
    separate = () if has_f else names_in
    operands = [scal, inp, f_recv, cot, b_recv, gains, shifts, fg, fs, pb, ub, wqk, wv, wout, wup, wdown]
    operands += [state[n] for n in separate] + [seq]
    base = len(operands)
    operands += [state[n] for n in alias]
    scratch = kernel_scratch(has_f, has_b)

    def body(*refs):
        if has_f and has_b:
            at = base + len(alias)
            by_name = dict(zip(outs, refs[at : at + len(outs)]))
            refs = refs[: base - 1] + tuple(by_name[n] for n in names_in) + refs[base - 1 :]
        layer_kernel(step, has_f, has_b, len(alias), names_in, *refs)

    got = pl.pallas_call(
        body,
        name="layer_" + "f" * has_f + "b" * has_b,
        out_shape=out_shape,
        in_specs=[SM] + [ANY] * (len(operands) - 1),
        out_specs=[ANY] * len(outs),
        scratch_shapes=[pltpu.VMEM(s, t) for _, s, t in scratch] + [pltpu.SemaphoreType.DMA((48,))],
        input_output_aliases={base + i: outs.index(n) for i, n in enumerate(alias)},
        compiler_params=pltpu.CompilerParams(vmem_limit_bytes=VMEM_ALL),
        cost_estimate=LIGHT,
    )(*operands)
    got = dict(zip(outs, got))
    state = dict(state)
    state.update({n: a for n, a in got.items() if n not in ("res", "send")})
    return got.get("res"), got.get("send"), state


TOK = MICRO * ROWS
WIDE = 768
SIDE = 128
ORDER = ("down", "up0", "up1", "att0", "att1", "down", "up0", "up1", "up0", "att0", "up1", "att1", "att0", "att1")


def grad_down_kernel(scal, hn, cot, q0, q1, q2, send, keep, hn_v, gy, out, sems):
    core = scal[0]
    half, rows = send.shape[0], send.shape[1]
    per = half * 2 * rows // (FF // WIDE) // (2 * rows)
    own = [pltpu.make_async_copy(q, gy.at[pl.ds(i * ROWS, ROWS)], sems.at[i]) for i, q in enumerate((q0, q1, q2))]
    given = pltpu.make_async_copy(cot, gy, sems.at[0])

    def load(g):
        at = aligned(g, WIDE)
        return pltpu.make_async_copy(hn.at[:, at], hn_v.at[:, at], sems.at[4 + g])

    def store(g):
        at = pl.ds(g * per, per)
        return (
            pltpu.make_async_copy(out.at[0, at], send.at[at], sems.at[8 + g]),
            pltpu.make_async_copy(out.at[1, at], keep.at[at], sems.at[12 + g]),
        )

    @pl.when(scal[1] == 0)
    def _():
        for c in own:
            c.start()

    @pl.when(scal[1] != 0)
    def _():
        given.start()

    for g in range(FF // WIDE):
        load(g).start()

    @pl.when(scal[1] == 0)
    def _():
        for c in own:
            c.wait()

    @pl.when(scal[1] != 0)
    def _():
        given.wait()

    def group(g, _):
        load(g).wait()
        for k in range(per):
            j = g * per + k
            r = dot_tn(hn_v[:, aligned(j, 2 * rows)], gy[...])
            out[1 - core, j] = r[:rows].astype(BF16)
            out[core, j] = r[rows:].astype(BF16)
        for c in store(g):
            c.start()
        return 0

    lax.fori_loop(0, FF // WIDE, group, 0)
    for g in range(FF // WIDE):
        for c in store(g):
            c.wait()


def down_call(scal, hn, cot, qs, n_dp):
    rows = FF // n_dp
    half = n_dp // 2
    shape = jax.ShapeDtypeStruct((half, rows, D), BF16)
    return pl.pallas_call(
        grad_down_kernel,
        name="grad_down",
        out_shape=[shape, shape],
        in_specs=[SM] + [ANY] * 5,
        out_specs=[ANY] * 2,
        scratch_shapes=[
            pltpu.VMEM((TOK, FF), BF16),
            pltpu.VMEM((TOK, D), BF16),
            pltpu.VMEM((2, half, rows, D), BF16),
            pltpu.SemaphoreType.DMA((16,)),
        ],
        compiler_params=pltpu.CompilerParams(vmem_limit_bytes=VMEM_ALL),
        cost_estimate=LIGHT,
    )(scal, hn.reshape(TOK, FF), cot.reshape(TOK, D), *qs)


def wide_kernel(n_left, n_right, parts, extra, *refs):
    n_in = 1 + n_left + n_right + extra
    scal, lefts, rights = refs[0], refs[1 : 1 + n_left], refs[1 + n_left : 1 + n_left + n_right]
    dsts = refs[n_in:][: 2 * parts]
    left_v, right_v, turned, out, sems = refs[n_in + 2 * parts :][:5]
    core = scal[0]
    half, rows = out.shape[1], out.shape[2]
    groups = right_v.shape[1] // WIDE
    per = groups // parts
    sources = [(r, k) for r in rights for k in range(r.shape[1] // WIDE)]
    left_copies = [pltpu.make_async_copy(x, left_v.at[i], sems.at[i]) for i, x in enumerate(lefts)]
    for c in left_copies:
        c.start()
    loads = []
    for g, (r, k) in enumerate(sources):
        c = pltpu.make_async_copy(r.at[:, pl.ds(k * WIDE, WIDE)], right_v.at[:, pl.ds(g * WIDE, WIDE)], sems.at[2 + g])
        c.start()
        loads.append(c)
    if extra:
        side_v = refs[-1]
        side_copy = pltpu.make_async_copy(refs[n_in - 1], side_v, sems.at[15])
        side_copy.start()
    for i, c in enumerate(left_copies):
        c.wait()
        turned[i] = left_v[i].T

    def put(r, at):
        for j in range(half):
            out[1 - core, j, :, at] = r[2 * j * rows : (2 * j + 1) * rows].astype(BF16)
            out[core, j, :, at] = r[(2 * j + 1) * rows : (2 * j + 2) * rows].astype(BF16)

    def product(g, _):
        at = aligned(g, WIDE)
        which = 0 if n_left == 1 else jnp.where(g >= groups - 1, 1, 0)
        put(dot_nn(turned[which], right_v[:, at]), at)
        return 0

    if extra:
        side_copy.wait()
        put(side_v[...], pl.ds(groups * WIDE, SIDE))
    stores = []
    for p in range(parts):
        for g in range(p * per, (p + 1) * per):
            loads[g].wait()
        lax.fori_loop(p * per, (p + 1) * per, product, 0)
        width = dsts[2 * p].shape[2]
        for side in range(2):
            c = pltpu.make_async_copy(
                out.at[side, :, :, pl.ds(p * per * WIDE, width)], dsts[2 * p + side], sems.at[6 + 2 * p + side]
            )
            c.start()
            stores.append(c)
    for c in stores:
        c.wait()


def wide_call(name, scal, lefts, rights, parts, n_dp, extra=None):
    rows = D // n_dp
    half = n_dp // 2
    cols = sum(r.shape[1] for r in rights)
    widths = [cols // parts] * parts
    if extra is not None:
        widths[-1] += SIDE
    shapes = [jax.ShapeDtypeStruct((half, rows, w), BF16) for w in widths for _ in range(2)]
    more = [] if extra is None else [extra]
    return pl.pallas_call(
        functools.partial(wide_kernel, len(lefts), len(rights), parts, len(more)),
        name=name,
        out_shape=shapes,
        in_specs=[SM] + [ANY] * (len(lefts) + len(rights) + len(more)),
        out_specs=[ANY] * (2 * parts),
        scratch_shapes=[
            pltpu.VMEM((len(lefts), TOK, D), BF16),
            pltpu.VMEM((TOK, cols), BF16),
            pltpu.VMEM((len(lefts), D, TOK), BF16),
            pltpu.VMEM((2, half, rows, sum(widths)), BF16),
            pltpu.SemaphoreType.DMA((16,)),
        ]
        + [pltpu.VMEM((D, SIDE), F32)] * len(more),
        compiler_params=pltpu.CompilerParams(vmem_limit_bytes=VMEM_ALL),
        cost_estimate=HEAVY,
    )(scal, *lefts, *rights, *more)


def merge_kernel(mine, ka, ga, kb, gb, send, keep):
    send[...] = (ka[...].astype(F32) + ga[...].astype(F32)).astype(BF16)
    keep[...] = (kb[...].astype(F32) + gb[...].astype(F32)).astype(BF16)


def merge(keep, got, mine):
    count, rows, cols = keep.shape
    shape = jax.ShapeDtypeStruct((count // 2, rows, cols), BF16)
    other = pl.BlockSpec((None, None, rows, cols), lambda i, m: (i, 1 - m[0], 0, 0))
    own = pl.BlockSpec((None, None, rows, cols), lambda i, m: (i, m[0], 0, 0))
    out = pl.BlockSpec((None, rows, cols), lambda i, m: (i, 0, 0))
    keep, got = (t.reshape(count // 2, 2, rows, cols) for t in (keep, got))
    return pl.pallas_call(
        merge_kernel,
        name="merge_halves",
        grid_spec=pltpu.PrefetchScalarGridSpec(
            num_scalar_prefetch=1, grid=(count // 2,), in_specs=[other, other, own, own], out_specs=[out, out]
        ),
        out_shape=[shape, shape],
        compiler_params=pltpu.CompilerParams(vmem_limit_bytes=VMEM_ALL),
        cost_estimate=HEAVY,
    )(mine, keep, got, keep, got)


def swap(x, bit, n_dp):
    return lax.ppermute(x, "dp", [(i, i ^ bit) for i in range(n_dp)])


def after(x, *others):
    return lax.optimization_barrier((x,) + others)[0]


class Exchange:
    def __init__(self, n_dp):
        self.n_dp = n_dp
        self.me = lax.axis_index("dp")
        self.last = None

    def step(self, chunk):
        send, keep, bit = chunk
        mine = (self.me // (2 * bit) % 2).astype(jnp.int32)[None]
        if self.last is not None:
            mine = after(mine, *self.last)
        self.last = merge(keep, swap(send, bit, self.n_dp), mine)
        return (*self.last, 2 * bit)

    def finish(self, chunk):
        send, keep, bit = chunk
        got = swap(send, bit, self.n_dp)
        return keep[0].astype(F32) + got[0].astype(F32)


def token_product(left, right):
    left, right = (t.reshape(TOK, t.shape[-1]) for t in (left, right))
    return lax.psum_scatter(dot_tn(left, right), "dp", scatter_dimension=0, tiled=True)


def token_sum(rows):
    return lax.psum_scatter(rows, "dp", scatter_dimension=1, tiled=True)


def shifted(x, by):
    length = lax.axis_size("section")
    pairs = [(i, i + by) for i in range(length) if 0 <= i + by < length]
    return lax.ppermute(x, "section", pairs)


def local(n_dp, inputs, out_cotangent, sequence_ids, *raw):
    params = raw[:5] + tuple(jnp.transpose(t, (1, 0, 2)) for t in raw[5:7]) + raw[7:]
    sec = lax.axis_index("section")
    me = lax.axis_index("dp")
    inp = inputs.reshape(MICRO, ROWS, D)
    cot = out_cotangent.reshape(MICRO, ROWS, D)
    seq = sequence_ids

    def code(f, b):
        mb = next((m for m in (f, b) if m is not None), 0)
        return [int(f is not None), int(b is not None), mb]

    plan = [(0, None, None, None), (1, None, None, None), (2, None, 0, 0), (None, None, 1, 1)]
    plan += [(None, 0, 2, 2), (None, 1, None, None), (None, 2, None, None)]
    first = [x for f0, b0, _, _ in plan for x in code(f0, b0)] + [0]
    second = [x for _, _, f1, b1 in plan for x in code(f1, b1)] + [1]
    table = jnp.where(sec == 0, jnp.array(first, jnp.int32), jnp.array(second, jnp.int32))
    none = inp
    state = {}

    def run(step, f_recv=none, b_recv=none, wait_for=()):
        nonlocal state
        f0, b0, f1, b1 = plan[step]
        has_f, has_b = f0 is not None or f1 is not None, b0 is not None or b1 is not None
        scal = after(table, *wait_for) if wait_for else table
        res, send, state = layer_call(step, scal, has_f, has_b, inp, f_recv, cot, b_recv, seq, params, state)
        return res, send

    r0, _ = run(0)
    p0 = shifted(r0, 1)
    r1, _ = run(1)
    p1 = shifted(r1, 1)
    r2, g0 = run(2, f_recv=p0)
    p2 = shifted(r2, 1)
    q0 = shifted(g0, -1)
    _, g1 = run(3, f_recv=p1)
    q1 = shifted(g1, -1)
    _, g2 = run(4, f_recv=p2, b_recv=q0)
    q2 = shifted(g2, -1)
    run(5, b_recv=q1)
    core = jnp.stack([me % 2, sec]).astype(jnp.int32)
    blocks = n_dp == 16
    done = ()
    if blocks:
        ex = Exchange(n_dp)
        down = ex.step((*down_call(after(core, state["gml"]), state["hn"], cot, (q0, q1, q2), n_dp), 1))
        done = ex.last
    run(6, b_recv=q2, wait_for=done)
    vec = jnp.sum(state["vec"], axis=0)
    vecf = jnp.sum(state["vecf"], axis=0)
    n1, n2 = D // n_dp, FF // n_dp
    if blocks:
        flat = {n: state[n].reshape(TOK, state[n].shape[-1]) for n in ("ffn_in", "dh", "normed", "mnormed", "gqkv", "gml")}
        side = [vec[:10].T, vecf[:3].reshape(3, n_dp, n2 // n1, n1).transpose(1, 3, 0, 2).reshape(D, -1)]
        used = 10 + 3 * (n2 // n1)
        side = jnp.concatenate(side + [jnp.zeros((D, SIDE - used), F32)], axis=1)
        att = wide_call("grad_attn", core, (flat["normed"], flat["mnormed"]), (flat["gqkv"], flat["gml"]), 2, n_dp)
        up = wide_call("grad_up", after(core, att[0]), (flat["ffn_in"],), (flat["dh"],), 2, n_dp, side)
        chunk = {"down": down}
        chunk.update({n: (*t, 1) for n, t in (("up0", up[:2]), ("up1", up[2:]), ("att0", att[:2]), ("att1", att[2:]))})
        ex.last = ex.last + up[:1]
        for n in ORDER:
            chunk[n] = ex.step(chunk[n])
        g_down, g_up0, g_up1, g_qk, g_vo = (ex.finish(chunk[n]) for n in ("down", "up0", "up1", "att0", "att1"))
        g_up = jnp.concatenate([g_up0, g_up1[:, : FF // 2]], axis=1)
        g_value, g_out = g_vo[:, :D], g_vo[:, D:]
        g_side = g_up1[:, FF // 2 : FF // 2 + used]
        va = g_side[:, :10].T
        vb = g_side[:, 10:].reshape(n1, 3, n2 // n1).transpose(1, 2, 0).reshape(3, n2)
    else:
        gy = jnp.where(sec == 0, jnp.stack([q0, q1, q2]), cot)
        g_down = token_product(state["hn"], gy)
        g_up = token_product(state["ffn_in"], state["dh"])
        g_attn = token_product(state["normed"], state["gqkv"])
        g_qk, g_value = g_attn[:, : 2 * D], g_attn[:, 2 * D :]
        g_out = token_product(state["mnormed"], state["gml"])
        va = token_sum(vec[:10])
        vb = token_sum(vecf[:3])
    rows = MICRO * ROWS
    return (
        state["louts"].reshape(1, rows, D),
        state["igr"].reshape(1, rows, D),
        g_qk[None],
        g_value[None],
        g_out[None],
        g_up[None],
        g_down[None],
        va[0:3][None],
        va[3:6][None],
        vb[0:1],
        vb[1:2],
        va[6:10][None],
        vb[2:3],
    )


def solution(mesh):
    in_specs = (
        P("dp", None),
        P("dp", None),
        P("dp", None),
        P("section", None, None),
        P("section", None, None),
        P("section", None, None),
        P("section", None, None),
        P("section", None, None),
        P("section", None, None),
        P("section", None, None),
        P("section", None),
        P("section", None),
        P("section", None, None),
        P("section", None),
    )
    out_specs = (
        P("section", "dp", None),
        P("section", "dp", None),
        P("section", "dp", None),
        P("section", "dp", None),
        P("section", "dp", None),
        P("section", "dp", None),
        P("section", "dp", None),
        P("section", None, "dp"),
        P("section", None, "dp"),
        P("section", "dp"),
        P("section", "dp"),
        P("section", None, "dp"),
        P("section", "dp"),
    )
    body = functools.partial(local, mesh.shape["dp"])
    return jax.shard_map(body, mesh=mesh, in_specs=in_specs, out_specs=out_specs, check_vma=False)
```

```python
import functools

import jax
import jax.numpy as jnp
from jax import lax
from jax.experimental import pallas as pl
from jax.experimental.pallas import tpu as pltpu
from jax.sharding import PartitionSpec as P

D = 768
HEADS = 12
HEAD_DIM = 64
FF = 3072
ROWS = 256
MICRO = 3
EPS = 1e-05
MASKED = -1e30
CH = 768
N_CH = FF // CH
UNROLL_ATT_F = 6
UNROLL_ATT_B = 2
UNROLL_UP = 2
UNROLL_DOWN = 2
UNROLL_B1 = 2
UNROLL_B2 = 2
VMEM_ALL = 63 << 20
LIGHT = pl.CostEstimate(flops=1000, bytes_accessed=1000, transcendentals=0)
STEPS = 7
HEAVY = pl.CostEstimate(flops=2 * 10**10, bytes_accessed=10 << 20, transcendentals=0)
PAIRS = HEADS // 2
F32 = jnp.float32
BF16 = jnp.bfloat16
ANY = pl.BlockSpec(memory_space=pl.ANY)
VM = pl.BlockSpec(memory_space=pltpu.VMEM)
SM = pl.BlockSpec(memory_space=pltpu.SMEM)


def dot_nn(a, b):
    return lax.dot_general(a, b, (((1,), (0,)), ((), ())), preferred_element_type=F32)


def dot_nt(a, b):
    return lax.dot_general(a, b, (((1,), (1,)), ((), ())), preferred_element_type=F32)


def dot_tn(a, b):
    return lax.dot_general(a, b, (((0,), (0,)), ((), ())), preferred_element_type=F32)


def center_spread(v):
    c = v - jnp.mean(v, axis=-1, keepdims=True)
    r = lax.rsqrt(jnp.mean(c * c, axis=-1, keepdims=True) + EPS)
    return c, r


def norm(v, gain, shift):
    c, r = center_spread(v)
    return c * r * gain + shift


def norm_back(grad, v, gain):
    c, r = center_spread(v)
    x = c * r
    h = grad * gain
    back = r * (h - jnp.mean(h, axis=-1, keepdims=True) - x * jnp.mean(h * x, axis=-1, keepdims=True))
    return back, colsum(grad * x), colsum(grad)


def colsum(v):
    return jnp.sum(v, axis=0, keepdims=True)


def lane_fold(v):
    total = v[:, :128]
    for k in range(1, v.shape[1] // 128):
        total = total + v[:, k * 128 : (k + 1) * 128]
    return total


def same_bias(seq_row):
    rows = jnp.broadcast_to(seq_row.astype(F32), (ROWS, ROWS))
    return jnp.where(rows == rows.T, 0.0, MASKED)


def aligned(i, size):
    return pl.ds(pl.multiple_of(i * size, size), size)


SAVED = (
    ("src", D, BF16),
    ("qkv", 3 * D, BF16),
    ("mixed", D, BF16),
    ("middle", D, BF16),
    ("xh", FF, BF16),
    ("gp", FF, BF16),
    ("rst", 128, F32),
)
F_OUT = (
    ("normed", D, BF16),
    ("mnormed", D, BF16),
    ("ffn_in", D, BF16),
    ("hn", FF, BF16),
    ("louts", D, BF16),
)
B_OUT = (
    ("dh", FF, BF16),
    ("gml", D, BF16),
    ("gqkv", 3 * D, BF16),
    ("igr", D, BF16),
    ("vec", D, F32),
    ("vecf", FF, F32),
)
STATE = SAVED + F_OUT + B_OUT
SMALL = (("gains", 3, D), ("shifts", 3, D), ("fg", 1, FF), ("fs", 1, FF), ("pb", 4, D), ("ub", 1, FF))
WEIGHTS = (("wqk", D, 2 * D), ("wv", D, D), ("wout", D, D), ("wup", D, FF), ("wdown", FF, D))


def rows_of(name):
    return {"vec": 16, "vecf": 8}.get(name, ROWS)


def inner_forward(v, cp, wait):
    normed_v, qkv, mid, act = v["normed"], v["qkv"], v["mid"], v["act"]
    gains, shifts, fg, fs, pb, ub = (v[n[0]] for n in SMALL)
    u = v["src"][...].astype(F32)
    normed_v[...] = norm(u, gains[0:1], shifts[0:1]).astype(BF16)
    cp.save("normed")
    wait("wqk", "wv")
    cp.load_late("wout", "wup")

    def project(i, _):
        at = aligned(i, 768)
        x = dot_nn(normed_v[...], v["wqkv"][:, at]) + v["qkvb"][0:1, at]
        qkv[:, at] = (x * jnp.where(i == 0, 0.125, 1.0)).astype(BF16)
        return 0

    lax.fori_loop(0, 3, project, 0)
    cp.save_kept("qkv")
    low = lax.broadcasted_iota(jnp.int32, (ROWS, 128), 1) < HEAD_DIM

    def pair(j, _):
        q2 = qkv[:, aligned(j, 128)]
        k2 = qkv[:, aligned(j + PAIRS, 128)]
        v2 = qkv[:, aligned(j + 2 * PAIRS, 128)]
        zero = jnp.zeros_like(k2)
        one = jnp.ones_like(v2)
        sums = []
        for first in (True, False):
            kh = jnp.where(low, k2, zero) if first else jnp.where(low, zero, k2)
            vh = jnp.where(low, v2, one) if first else jnp.where(low, one, v2)
            scores = dot_nt(q2, kh) + v["bias"][...]
            lifted = jnp.exp(scores - jnp.max(scores, axis=-1, keepdims=True)).astype(BF16)
            sums.append(dot_nn(lifted, vh))
        top = jnp.where(low, sums[0], sums[1])
        den = pltpu.roll(jnp.where(low, sums[1], sums[0]), 64, 1)
        mid[:, aligned(j, 128)] = top / den
        return 0

    lax.fori_loop(0, PAIRS, pair, 0, unroll=UNROLL_ATT_F)
    cp.load_late("wdown")
    mixed = mid[...]
    v["mixed"][...] = mixed.astype(BF16)
    cp.save_kept("mixed")
    mnormed = norm(mixed, gains[1:2], shifts[1:2]).astype(BF16)
    v["mnormed"][...] = mnormed
    cp.save("mnormed")
    wait("wout")
    middle = v["src"][...].astype(F32) + dot_nn(mnormed, v["wout"][...]) + pb[2:3]
    mid[...] = middle
    v["middle"][...] = middle.astype(BF16)
    cp.save_kept("middle")
    cp.save_kept("src")
    v["ffn_in"][...] = norm(middle, gains[2:3], shifts[2:3]).astype(BF16)
    cp.save("ffn_in")
    wait("wup")

    def up(i, total):
        at = aligned(i, CH)
        h = dot_nn(v["ffn_in"][...], v["wup"][:, at]) + ub[:, at]
        cdf = 0.5 + 0.5 * lax.erf(h * 0.7071067811865476)
        a = h * cdf
        act[:, at] = a
        pdf = jnp.exp2(h * h * -0.7213475204444817 - 1.3257480647361594)
        v["gp"][:, at] = (cdf + h * pdf).astype(BF16)
        return total + lane_fold(a)

    total = lax.fori_loop(0, N_CH, up, jnp.zeros((ROWS, 128), F32), unroll=UNROLL_UP)
    cp.save_kept("gp")
    mean = jnp.sum(total, axis=-1, keepdims=True) * (1.0 / FF)

    def spread(i, total):
        c = act[:, aligned(i, CH)] - mean
        return total + lane_fold(c * c)

    total = lax.fori_loop(0, N_CH, spread, jnp.zeros((ROWS, 128), F32))
    r = lax.rsqrt(jnp.sum(total, axis=-1, keepdims=True) * (1.0 / FF) + EPS)
    v["rst"][...] = jnp.broadcast_to(r, (ROWS, 128))
    cp.save_kept("rst")
    wait("wdown")
    v["acc"][...] = mid[...] + pb[3:4]

    def down(i, _):
        at = aligned(i, CH)
        x = (act[:, at] - mean) * r
        v["xh"][:, at] = x.astype(BF16)
        hn = (x * fg[:, at] + fs[:, at]).astype(BF16)
        v["hn"][:, at] = hn
        v["acc"][...] += dot_nn(hn, v["wdown"][at, :])
        return 0

    lax.fori_loop(0, N_CH, down, 0, unroll=UNROLL_DOWN)
    v["louts"][...] = v["acc"][...].astype(BF16)
    cp.save("louts")
    cp.save("res")
    cp.save("hn")
    cp.save_kept("xh")


def inner_backward(v, cp, wait, ready):
    gains, fg = v["gains"], v["fg"]
    act, acc, mid, gy_b, xh, gp, qkv, gqkv = (v[n] for n in ("act", "acc", "mid", "gy", "xh", "gp", "qkv", "gqkv"))
    vec, vecf = v["vec"], v["vecf"]
    vec[9:10] = colsum(gy_b[...].astype(F32))
    wait("wdown")
    ready("xh")

    def first(i, totals):
        at = aligned(i, CH)
        g = dot_nt(gy_b[...], v["wdown"][at, :])
        x = xh[:, at].astype(F32)
        gx = g * x
        vecf[0:1, at] = colsum(gx)
        vecf[1:2, at] = colsum(g)
        h = g * fg[:, at]
        act[:, at] = h
        return totals[0] + lane_fold(h), totals[1] + lane_fold(h * x)

    zeros = jnp.zeros((ROWS, 128), F32)
    t1, t2 = lax.fori_loop(0, N_CH, first, (zeros, zeros), unroll=UNROLL_B1)
    m1 = jnp.sum(t1, axis=-1, keepdims=True) * (1.0 / FF)
    m2 = jnp.sum(t2, axis=-1, keepdims=True) * (1.0 / FF)
    ready("gp", "rst")
    wait("wup")
    r = v["rst"][:, 0:1]
    acc[...] = jnp.zeros_like(acc)

    def second(i, _):
        at = aligned(i, CH)
        x = xh[:, at].astype(F32)
        d = (act[:, at] - m1 - x * m2) * r * gp[:, at].astype(F32)
        vecf[2:3, at] = colsum(d)
        low_d = d.astype(BF16)
        v["dh"][:, at] = low_d
        acc[...] += dot_nt(low_d, v["wup"][:, at])
        return 0

    lax.fori_loop(0, N_CH, second, 0, unroll=UNROLL_B2)
    cp.save("dh")
    cp.save("vecf")
    ready("middle")
    back, v_gain, v_shift = norm_back(acc[...], v["middle"][...].astype(F32), gains[2:3])
    vec[2:3] = v_gain
    vec[5:6] = v_shift
    gm = gy_b[...].astype(F32) + back
    mid[...] = gm
    gml_v = gm.astype(BF16)
    v["gml"][...] = gml_v
    cp.save("gml")
    vec[8:9] = colsum(gm)
    wait("wout")
    ready("mixed")
    back, v_gain, v_shift = norm_back(dot_nt(gml_v, v["wout"][...]), v["mixed"][...].astype(F32), gains[1:2])
    vec[1:2] = v_gain
    vec[4:5] = v_shift
    v["gmix"][...] = back.astype(BF16)
    ready("qkv")
    low = lax.broadcasted_iota(jnp.int32, (ROWS, 128), 1) < HEAD_DIM

    def pair(j, _):
        q2 = qkv[:, aligned(j, 128)]
        k2 = qkv[:, aligned(j + PAIRS, 128)]
        v2 = qkv[:, aligned(j + 2 * PAIRS, 128)]
        g2 = v["gmix"][:, aligned(j, 128)]
        zero = jnp.zeros_like(k2)
        gq = gk = gv = None
        for head in range(2):

            def half(t):
                return jnp.where(low, t, zero) if head == 0 else jnp.where(low, zero, t)

            kh, vh, qh, gh = half(k2), half(v2), half(q2), half(g2)
            st = dot_nt(kh, q2) + v["bias"][...]
            e = jnp.exp(st - jnp.max(st, axis=0, keepdims=True))
            p = e * (1.0 / jnp.sum(e, axis=0, keepdims=True))
            gp_t = dot_nt(vh, g2)
            inner = jnp.sum(p * gp_t, axis=0, keepdims=True)
            gs = (p * (gp_t - inner)).astype(BF16)
            a = dot_nn(p.astype(BF16), gh)
            b = dot_nn(gs, qh)
            c = dot_tn(gs, kh * 0.125)
            gv = a if gv is None else gv + a
            gk = b if gk is None else gk + b
            gq = c if gq is None else gq + c
        gqkv[:, aligned(j, 128)] = gq.astype(BF16)
        gqkv[:, aligned(j + PAIRS, 128)] = gk.astype(BF16)
        gqkv[:, aligned(j + 2 * PAIRS, 128)] = gv.astype(BF16)
        vec[6:7, aligned(j, 128)] = colsum(gq)
        vec[7:8, aligned(j, 128)] = colsum(gv)
        return 0

    lax.fori_loop(0, PAIRS, pair, 0, unroll=UNROLL_ATT_B)
    cp.save("gqkv")
    wait("wqk", "wv")
    ready("src")

    def back_chunk(i, _):
        at = aligned(i, 768)
        acc[...] += dot_nt(gqkv[:, at], v["wqkv"][:, at])
        return 0

    acc[...] = jnp.zeros_like(acc)
    lax.fori_loop(0, 3, back_chunk, 0)
    back, v_gain, v_shift = norm_back(acc[...], v["src"][...].astype(F32), gains[0:1])
    vec[0:1] = v_gain
    vec[3:4] = v_shift
    v["igr"][...] = (mid[...] + back).astype(BF16)
    cp.save("send")
    cp.save("igr")
    cp.save("vec")


class Traffic:
    def __init__(self, v, hbm, sems, mb, both):
        self.v, self.hbm, self.sems, self.mb, self.both = v, hbm, sems, mb, both
        self.at = {}
        self.kept = []
        self.late = True

    def sem(self, key):
        return self.sems.at[self.at.setdefault(key, len(self.at))]

    def weight(self, name):
        dst = self.v[name] if name in ("wout", "wup", "wdown") else None
        if name == "wqk":
            dst = self.v["wqkv"].at[:, pl.ds(0, 2 * D)]
        if name == "wv":
            dst = self.v["wqkv"].at[:, pl.ds(2 * D, D)]
        return pltpu.make_async_copy(self.hbm[name].at[0], dst, self.sem(name))

    def load_late(self, *names):
        for n in names:
            self.weight(n).start()

    def out(self, name):
        source = {"res": "louts", "send": "igr"}.get(name, name)
        dst = self.hbm[name] if name in ("res", "send") else self.hbm["o_" + name].at[self.mb]
        return pltpu.make_async_copy(self.v[source], dst, self.sem("o_" + name))

    def save(self, name):
        copy = self.out(name)
        copy.start()
        self.kept.append((name, False))

    def save_kept(self, name):
        copy = self.out(name)
        self.kept.append((name, True))

        @pl.when(jnp.logical_not(self.both))
        def _():
            copy.start()

    def finish(self):
        for name, conditional in self.kept:
            if conditional:

                @pl.when(jnp.logical_not(self.both))
                def _(name=name):
                    self.out(name).wait()
            else:
                self.out(name).wait()
        self.kept = []


def first_of(ref):
    if len(ref.shape) == 3:
        return ref.at[:, 0] if ref.shape[1] == 1 else ref.at[0]
    return ref


def layer_kernel(step, has_f, has_b, n_alias, names_in, *refs):
    n_in = 5 + len(SMALL) + len(WEIGHTS)
    scal, inp_all, f_recv, cot_all, b_recv = refs[:5]
    hbm = dict(zip([n[0] for n in SMALL + WEIGHTS], refs[5:n_in]))
    k = n_in
    ins = dict(zip(names_in, refs[k : k + len(names_in)]))
    seq_h = refs[k + len(names_in)]
    k += len(names_in) + 1 + n_alias
    outs = kernel_outs(has_f, has_b)
    for name in outs:
        hbm["o_" + name if name not in ("res", "send") else name] = refs[k]
        k += 1
    v = dict(zip([n for n, _, _ in kernel_scratch(has_f, has_b)], refs[k:]))
    sems = refs[-1]
    do_f, do_b, mb, sec = scal[3 * step] == 1, scal[3 * step + 1] == 1, scal[3 * step + 2], scal[3 * STEPS]
    only_b = jnp.logical_and(do_b, jnp.logical_not(do_f))

    @pl.when(jnp.logical_or(do_f, do_b))
    def _():
        cp = Traffic(v, hbm, sems, mb, do_b)
        smalls = [pltpu.make_async_copy(first_of(hbm[n]), v[n], cp.sem(n)) for n, _, _ in SMALL]
        seq_copy = pltpu.make_async_copy(seq_h, v["seq"], cp.sem("seq"))
        first_in = pltpu.make_async_copy(first_of(f_recv), v["src"], cp.sem("in")) if has_f else None
        gy_in = pltpu.make_async_copy(first_of(b_recv), v["gy"], cp.sem("gy")) if has_b else None

        def pick(copy, other, own):
            @pl.when(own)
            def _():
                other.start()

            @pl.when(jnp.logical_not(own))
            def _():
                copy.start()

        loads = {n: pltpu.make_async_copy(ins[n].at[mb], v[n], cp.sem("i_" + n)) for n in names_in} if has_b else {}
        if has_f:

            @pl.when(do_f)
            def _():
                pick(first_in, pltpu.make_async_copy(inp_all.at[mb], v["src"], cp.sem("in")), sec == 0)
                cp.load_late("wqk", "wv")

        for c in smalls:
            c.start()
        seq_copy.start()
        if has_b:

            @pl.when(do_b)
            def _():
                pick(gy_in, pltpu.make_async_copy(cot_all.at[mb], v["gy"], cp.sem("gy")), sec != 0)

            @pl.when(only_b)
            def _():
                cp.load_late("wdown")
                for n in ("xh", "gp", "rst"):
                    loads[n].start()
                cp.load_late("wup")
                for n in ("middle", "mixed", "qkv", "src"):
                    loads[n].start()
                cp.load_late("wout", "wqk", "wv")

        seq_copy.wait()
        v["bias"][...] = same_bias(v["seq"][pl.ds(mb, 1), :])
        for c in smalls:
            c.wait()
        if has_f:

            @pl.when(do_f)
            def _():
                v["qkvb"][:, 0:D] = v["pb"][0:1]
                v["qkvb"][:, D : 2 * D] = jnp.zeros((1, D), F32)
                v["qkvb"][:, 2 * D :] = v["pb"][1:2]
                first_in.wait()

                def wait(*names):
                    for n in names:
                        cp.weight(n).wait()

                inner_forward(v, cp, wait)
                if not has_b:
                    cp.finish()

        if has_b:

            @pl.when(do_b)
            def _():
                gy_in.wait()

                def wait(*names):
                    @pl.when(only_b)
                    def _():
                        for n in names:
                            cp.weight(n).wait()

                def ready(*names):
                    @pl.when(only_b)
                    def _():
                        for n in names:
                            loads[n].wait()

                back = Traffic(v, hbm, sems, mb, do_b)
                back.at = cp.at
                inner_backward(v, back, wait, ready)
                back.finish()

            if has_f:

                @pl.when(do_f)
                def _():
                    cp.finish()


def kernel_outs(has_f, has_b):
    names = []
    if has_f:
        names += [n for n, _, _ in SAVED + F_OUT] + ["res"]
    if has_b:
        names += [n for n, _, _ in B_OUT] + ["send"]
    return names


def kernel_scratch(has_f, has_b):
    out = [(n, (r, c), F32) for n, r, c in SMALL]
    out += [("wqkv", (D, 3 * D), BF16)]
    out += [(n, (r, c), BF16) for n, r, c in WEIGHTS[2:]]
    out += [(n, (ROWS, c), t) for n, c, t in SAVED]
    if has_f:
        out += [(n, (ROWS, c), t) for n, c, t in F_OUT] + [("qkvb", (1, 3 * D), F32)]
    if has_b:
        out += [(n, (rows_of(n), c), t) for n, c, t in B_OUT]
        out += [("gy", (ROWS, D), BF16), ("gmix", (ROWS, D), BF16)]
    out += [("seq", (MICRO, ROWS), jnp.int32), ("bias", (ROWS, ROWS), F32)]
    out += [("act", (ROWS, FF), F32), ("acc", (ROWS, D), F32), ("mid", (ROWS, D), F32)]
    return out


def layer_call(step, scal, has_f, has_b, inp, f_recv, cot, b_recv, seq, params, state):
    wqk, wv, wout, wup, wdown, gains, shifts, fg, fs, pb, ub = params
    names_in = tuple(n for n, _, _ in SAVED) if has_b else ()
    outs = kernel_outs(has_f, has_b)
    alias = [n for n in outs if n in state]
    shapes = {n: (rows_of(n), c, t) for n, c, t in STATE}
    out_shape = []
    for n in outs:
        if n in ("res", "send"):
            out_shape.append(jax.ShapeDtypeStruct((ROWS, D), BF16))
        else:
            r, c, t = shapes[n]
            out_shape.append(jax.ShapeDtypeStruct((MICRO, r, c), t))
    separate = () if has_f else names_in
    operands = [scal, inp, f_recv, cot, b_recv, gains, shifts, fg, fs, pb, ub, wqk, wv, wout, wup, wdown]
    operands += [state[n] for n in separate] + [seq]
    base = len(operands)
    operands += [state[n] for n in alias]
    scratch = kernel_scratch(has_f, has_b)

    def body(*refs):
        if has_f and has_b:
            at = base + len(alias)
            by_name = dict(zip(outs, refs[at : at + len(outs)]))
            refs = refs[: base - 1] + tuple(by_name[n] for n in names_in) + refs[base - 1 :]
        layer_kernel(step, has_f, has_b, len(alias), names_in, *refs)

    got = pl.pallas_call(
        body,
        name="layer_" + "f" * has_f + "b" * has_b,
        out_shape=out_shape,
        in_specs=[SM] + [ANY] * (len(operands) - 1),
        out_specs=[ANY] * len(outs),
        scratch_shapes=[pltpu.VMEM(s, t) for _, s, t in scratch] + [pltpu.SemaphoreType.DMA((48,))],
        input_output_aliases={base + i: outs.index(n) for i, n in enumerate(alias)},
        compiler_params=pltpu.CompilerParams(vmem_limit_bytes=VMEM_ALL),
        cost_estimate=LIGHT,
    )(*operands)
    got = dict(zip(outs, got))
    state = dict(state)
    state.update({n: a for n, a in got.items() if n not in ("res", "send")})
    return got.get("res"), got.get("send"), state


TOK = MICRO * ROWS
WIDE = 768
SIDE = 128
ORDER = ("down", "up0", "up1", "att0", "att1", "down", "up0", "up1", "up0", "att0", "up1", "att1", "att0", "att1")


def grad_down_kernel(scal, hn, cot, q0, q1, q2, send, keep, hn_v, gy, out, sems):
    core = scal[0]
    half, rows = send.shape[0], send.shape[1]
    per = half * 2 * rows // (FF // WIDE) // (2 * rows)
    own = [pltpu.make_async_copy(q, gy.at[pl.ds(i * ROWS, ROWS)], sems.at[i]) for i, q in enumerate((q0, q1, q2))]
    given = pltpu.make_async_copy(cot, gy, sems.at[0])

    def load(g):
        at = aligned(g, WIDE)
        return pltpu.make_async_copy(hn.at[:, at], hn_v.at[:, at], sems.at[4 + g])

    def store(g):
        at = pl.ds(g * per, per)
        return (
            pltpu.make_async_copy(out.at[0, at], send.at[at], sems.at[8 + g]),
            pltpu.make_async_copy(out.at[1, at], keep.at[at], sems.at[12 + g]),
        )

    @pl.when(scal[1] == 0)
    def _():
        for c in own:
            c.start()

    @pl.when(scal[1] != 0)
    def _():
        given.start()

    for g in range(FF // WIDE):
        load(g).start()

    @pl.when(scal[1] == 0)
    def _():
        for c in own:
            c.wait()

    @pl.when(scal[1] != 0)
    def _():
        given.wait()

    def group(g, _):
        load(g).wait()
        for k in range(per):
            j = g * per + k
            r = dot_tn(hn_v[:, aligned(j, 2 * rows)], gy[...])
            out[1 - core, j] = r[:rows].astype(BF16)
            out[core, j] = r[rows:].astype(BF16)
        for c in store(g):
            c.start()
        return 0

    lax.fori_loop(0, FF // WIDE, group, 0)
    for g in range(FF // WIDE):
        for c in store(g):
            c.wait()


def down_call(scal, hn, cot, qs, n_dp):
    rows = FF // n_dp
    half = n_dp // 2
    shape = jax.ShapeDtypeStruct((half, rows, D), BF16)
    return pl.pallas_call(
        grad_down_kernel,
        name="grad_down",
        out_shape=[shape, shape],
        in_specs=[SM] + [ANY] * 5,
        out_specs=[ANY] * 2,
        scratch_shapes=[
            pltpu.VMEM((TOK, FF), BF16),
            pltpu.VMEM((TOK, D), BF16),
            pltpu.VMEM((2, half, rows, D), BF16),
            pltpu.SemaphoreType.DMA((16,)),
        ],
        compiler_params=pltpu.CompilerParams(vmem_limit_bytes=VMEM_ALL),
        cost_estimate=LIGHT,
    )(scal, hn.reshape(TOK, FF), cot.reshape(TOK, D), *qs)


def wide_kernel(n_left, n_right, parts, extra, *refs):
    n_in = 1 + n_left + n_right + extra
    scal, lefts, rights = refs[0], refs[1 : 1 + n_left], refs[1 + n_left : 1 + n_left + n_right]
    dsts = refs[n_in:][: 2 * parts]
    left_v, right_v, turned, out, sems = refs[n_in + 2 * parts :][:5]
    core = scal[0]
    half, rows = out.shape[1], out.shape[2]
    groups = right_v.shape[1] // WIDE
    per = groups // parts
    sources = [(r, k) for r in rights for k in range(r.shape[1] // WIDE)]
    left_copies = [pltpu.make_async_copy(x, left_v.at[i], sems.at[i]) for i, x in enumerate(lefts)]
    for c in left_copies:
        c.start()
    loads = []
    for g, (r, k) in enumerate(sources):
        c = pltpu.make_async_copy(r.at[:, pl.ds(k * WIDE, WIDE)], right_v.at[:, pl.ds(g * WIDE, WIDE)], sems.at[2 + g])
        c.start()
        loads.append(c)
    if extra:
        side_v = refs[-1]
        side_copy = pltpu.make_async_copy(refs[n_in - 1], side_v, sems.at[16])
        side_copy.start()
    for i, c in enumerate(left_copies):
        c.wait()
        turned[i] = left_v[i].T

    def put(r, at):
        for j in range(half):
            out[1 - core, j, :, at] = r[2 * j * rows : (2 * j + 1) * rows].astype(BF16)
            out[core, j, :, at] = r[(2 * j + 1) * rows : (2 * j + 2) * rows].astype(BF16)

    def store(g, p, side):
        return pltpu.make_async_copy(
            out.at[side, :, :, aligned(g, WIDE)],
            dsts[2 * p + side].at[:, :, aligned(g - p * per, WIDE)],
            sems.at[6 + 2 * g + side],
        )

    def product(g, _):
        at = aligned(g, WIDE)
        which = 0 if n_left == 1 else jnp.where(g >= groups - 1, 1, 0)
        pltpu.make_async_copy(right_v.at[:, at], right_v.at[:, at], sems.at[2 + g]).wait()
        put(dot_nn(turned[which], right_v[:, at]), at)
        for p in range(parts):

            @pl.when(g // per == p)
            def _(p=p):
                for side in range(2):
                    store(g, p, side).start()

        return 0

    stores = []
    if extra:
        side_copy.wait()
        put(side_v[...], pl.ds(groups * WIDE, SIDE))
        for side in range(2):
            c = pltpu.make_async_copy(
                out.at[side, :, :, pl.ds(groups * WIDE, SIDE)],
                dsts[2 * parts - 2 + side].at[:, :, pl.ds(per * WIDE, SIDE)],
                sems.at[14 + side],
            )
            c.start()
            stores.append(c)
    lax.fori_loop(0, groups, product, 0)
    stores += [store(g, g // per, side) for g in range(groups) for side in range(2)]
    for c in stores:
        c.wait()


def wide_call(name, scal, lefts, rights, parts, n_dp, extra=None):
    rows = D // n_dp
    half = n_dp // 2
    cols = sum(r.shape[1] for r in rights)
    widths = [cols // parts] * parts
    if extra is not None:
        widths[-1] += SIDE
    shapes = [jax.ShapeDtypeStruct((half, rows, w), BF16) for w in widths for _ in range(2)]
    more = [] if extra is None else [extra]
    return pl.pallas_call(
        functools.partial(wide_kernel, len(lefts), len(rights), parts, len(more)),
        name=name,
        out_shape=shapes,
        in_specs=[SM] + [ANY] * (len(lefts) + len(rights) + len(more)),
        out_specs=[ANY] * (2 * parts),
        scratch_shapes=[
            pltpu.VMEM((len(lefts), TOK, D), BF16),
            pltpu.VMEM((TOK, cols), BF16),
            pltpu.VMEM((len(lefts), D, TOK), BF16),
            pltpu.VMEM((2, half, rows, sum(widths)), BF16),
            pltpu.SemaphoreType.DMA((17,)),
        ]
        + [pltpu.VMEM((D, SIDE), F32)] * len(more),
        compiler_params=pltpu.CompilerParams(vmem_limit_bytes=VMEM_ALL),
        cost_estimate=HEAVY,
    )(scal, *lefts, *rights, *more)


def merge_kernel(mine, ka, ga, kb, gb, send, keep):
    send[...] = (ka[...].astype(F32) + ga[...].astype(F32)).astype(BF16)
    keep[...] = (kb[...].astype(F32) + gb[...].astype(F32)).astype(BF16)


def merge(keep, got, mine):
    count, rows, cols = keep.shape
    shape = jax.ShapeDtypeStruct((count // 2, rows, cols), BF16)
    other = pl.BlockSpec((None, None, rows, cols), lambda i, m: (i, 1 - m[0], 0, 0))
    own = pl.BlockSpec((None, None, rows, cols), lambda i, m: (i, m[0], 0, 0))
    out = pl.BlockSpec((None, rows, cols), lambda i, m: (i, 0, 0))
    keep, got = (t.reshape(count // 2, 2, rows, cols) for t in (keep, got))
    return pl.pallas_call(
        merge_kernel,
        name="merge_halves",
        grid_spec=pltpu.PrefetchScalarGridSpec(
            num_scalar_prefetch=1, grid=(count // 2,), in_specs=[other, other, own, own], out_specs=[out, out]
        ),
        out_shape=[shape, shape],
        compiler_params=pltpu.CompilerParams(vmem_limit_bytes=VMEM_ALL),
        cost_estimate=HEAVY,
    )(mine, keep, got, keep, got)


def swap(x, bit, n_dp):
    return lax.ppermute(x, "dp", [(i, i ^ bit) for i in range(n_dp)])


def after(x, *others):
    return lax.optimization_barrier((x,) + others)[0]


class Exchange:
    def __init__(self, n_dp):
        self.n_dp = n_dp
        self.me = lax.axis_index("dp")
        self.last = None

    def step(self, chunk):
        send, keep, bit = chunk
        mine = (self.me // (2 * bit) % 2).astype(jnp.int32)[None]
        if self.last is not None:
            mine = after(mine, *self.last)
        self.last = merge(keep, swap(send, bit, self.n_dp), mine)
        return (*self.last, 2 * bit)

    def finish(self, chunk):
        send, keep, bit = chunk
        got = swap(send, bit, self.n_dp)
        return keep[0].astype(F32) + got[0].astype(F32)


def token_product(left, right):
    left, right = (t.reshape(TOK, t.shape[-1]) for t in (left, right))
    return lax.psum_scatter(dot_tn(left, right), "dp", scatter_dimension=0, tiled=True)


def token_sum(rows):
    return lax.psum_scatter(rows, "dp", scatter_dimension=1, tiled=True)


def shifted(x, by):
    length = lax.axis_size("section")
    pairs = [(i, i + by) for i in range(length) if 0 <= i + by < length]
    return lax.ppermute(x, "section", pairs)


def local(n_dp, inputs, out_cotangent, sequence_ids, *raw):
    params = raw[:5] + tuple(jnp.transpose(t, (1, 0, 2)) for t in raw[5:7]) + raw[7:]
    sec = lax.axis_index("section")
    me = lax.axis_index("dp")
    inp = inputs.reshape(MICRO, ROWS, D)
    cot = out_cotangent.reshape(MICRO, ROWS, D)
    seq = sequence_ids

    def code(f, b):
        mb = next((m for m in (f, b) if m is not None), 0)
        return [int(f is not None), int(b is not None), mb]

    plan = [(0, None, None, None), (1, None, None, None), (2, None, 0, 0), (None, None, 1, 1)]
    plan += [(None, 0, 2, 2), (None, 1, None, None), (None, 2, None, None)]
    first = [x for f0, b0, _, _ in plan for x in code(f0, b0)] + [0]
    second = [x for _, _, f1, b1 in plan for x in code(f1, b1)] + [1]
    table = jnp.where(sec == 0, jnp.array(first, jnp.int32), jnp.array(second, jnp.int32))
    none = inp
    state = {}

    def run(step, f_recv=none, b_recv=none, wait_for=()):
        nonlocal state
        f0, b0, f1, b1 = plan[step]
        has_f, has_b = f0 is not None or f1 is not None, b0 is not None or b1 is not None
        scal = after(table, *wait_for) if wait_for else table
        res, send, state = layer_call(step, scal, has_f, has_b, inp, f_recv, cot, b_recv, seq, params, state)
        return res, send

    r0, _ = run(0)
    p0 = shifted(r0, 1)
    r1, _ = run(1)
    p1 = shifted(r1, 1)
    r2, g0 = run(2, f_recv=p0)
    p2 = shifted(r2, 1)
    q0 = shifted(g0, -1)
    _, g1 = run(3, f_recv=p1)
    q1 = shifted(g1, -1)
    _, g2 = run(4, f_recv=p2, b_recv=q0)
    q2 = shifted(g2, -1)
    run(5, b_recv=q1)
    core = jnp.stack([me % 2, sec]).astype(jnp.int32)
    blocks = n_dp == 16
    done = ()
    if blocks:
        ex = Exchange(n_dp)
        down = ex.step((*down_call(after(core, state["gml"]), state["hn"], cot, (q0, q1, q2), n_dp), 1))
        done = ex.last
    run(6, b_recv=q2, wait_for=done)
    vec = jnp.sum(state["vec"], axis=0)
    vecf = jnp.sum(state["vecf"], axis=0)
    n1, n2 = D // n_dp, FF // n_dp
    if blocks:
        flat = {n: state[n].reshape(TOK, state[n].shape[-1]) for n in ("ffn_in", "dh", "normed", "mnormed", "gqkv", "gml")}
        side = [vec[:10].T, vecf[:3].reshape(3, n_dp, n2 // n1, n1).transpose(1, 3, 0, 2).reshape(D, -1)]
        used = 10 + 3 * (n2 // n1)
        side = jnp.concatenate(side + [jnp.zeros((D, SIDE - used), F32)], axis=1)
        att = wide_call("grad_attn", core, (flat["normed"], flat["mnormed"]), (flat["gqkv"], flat["gml"]), 2, n_dp)
        up = wide_call("grad_up", after(core, att[0]), (flat["ffn_in"],), (flat["dh"],), 2, n_dp, side)
        chunk = {"down": down}
        chunk.update({n: (*t, 1) for n, t in (("up0", up[:2]), ("up1", up[2:]), ("att0", att[:2]), ("att1", att[2:]))})
        ex.last = ex.last + up[:1]
        for n in ORDER:
            chunk[n] = ex.step(chunk[n])
        g_down, g_up0, g_up1, g_qk, g_vo = (ex.finish(chunk[n]) for n in ("down", "up0", "up1", "att0", "att1"))
        g_up = jnp.concatenate([g_up0, g_up1[:, : FF // 2]], axis=1)
        g_value, g_out = g_vo[:, :D], g_vo[:, D:]
        g_side = g_up1[:, FF // 2 : FF // 2 + used]
        va = g_side[:, :10].T
        vb = g_side[:, 10:].reshape(n1, 3, n2 // n1).transpose(1, 2, 0).reshape(3, n2)
    else:
        gy = jnp.where(sec == 0, jnp.stack([q0, q1, q2]), cot)
        g_down = token_product(state["hn"], gy)
        g_up = token_product(state["ffn_in"], state["dh"])
        g_attn = token_product(state["normed"], state["gqkv"])
        g_qk, g_value = g_attn[:, : 2 * D], g_attn[:, 2 * D :]
        g_out = token_product(state["mnormed"], state["gml"])
        va = token_sum(vec[:10])
        vb = token_sum(vecf[:3])
    rows = MICRO * ROWS
    return (
        state["louts"].reshape(1, rows, D),
        state["igr"].reshape(1, rows, D),
        g_qk[None],
        g_value[None],
        g_out[None],
        g_up[None],
        g_down[None],
        va[0:3][None],
        va[3:6][None],
        vb[0:1],
        vb[1:2],
        va[6:10][None],
        vb[2:3],
    )


def solution(mesh):
    in_specs = (
        P("dp", None),
        P("dp", None),
        P("dp", None),
        P("section", None, None),
        P("section", None, None),
        P("section", None, None),
        P("section", None, None),
        P("section", None, None),
        P("section", None, None),
        P("section", None, None),
        P("section", None),
        P("section", None),
        P("section", None, None),
        P("section", None),
    )
    out_specs = (
        P("section", "dp", None),
        P("section", "dp", None),
        P("section", "dp", None),
        P("section", "dp", None),
        P("section", "dp", None),
        P("section", "dp", None),
        P("section", "dp", None),
        P("section", None, "dp"),
        P("section", None, "dp"),
        P("section", "dp"),
        P("section", "dp"),
        P("section", None, "dp"),
        P("section", "dp"),
    )
    body = functools.partial(local, mesh.shape["dp"])
    return jax.shard_map(body, mesh=mesh, in_specs=in_specs, out_specs=out_specs, check_vma=False)
```
